256 devices in a mesh: box: 16 (over y_lo, z), theta: 4 (over y_hi, core), phi: 4 (over x).
Axes of the slice: x: 4, y: 4 (y_hi: 2, y_lo: 2; y = y_hi * 2 + y_lo), z: 8, core: 2. Of those that a mesh axis runs over, the one named last changes fastest.
Arguments:
- coeffs: bfloat16 [2048, 2, 128, 256], P(('box', 'theta', 'phi')), may hold values from -6 to 6
- near_blocks: bfloat16 [2048, 12, 2, 128, 128], P(('box', 'theta', 'phi')), may hold values from -0.109375 to 0.109375
- near_ids: int32 [2048, 12], P(('box', 'theta', 'phi')), may hold values from 0 to 2047, as said below
- near_count: int32 [2048], P(('box', 'theta', 'phi')), may hold values from 3 to 12, as said below
- radiation: bfloat16 [2048, 2, 128, 128], P(('box', 'theta', 'phi')), may hold values from -0.5 to 0.5
- partners: int32 [256, 16], P('box'), may hold values from 0 to 255, as said below
- vector_ids: int32 [256, 16], P('box'), may hold values from 0 to 315
- pair_count: int32 [256], P('box'), may hold values from 4 to 16, as said below
- translation: bfloat16 [316, 2, 16, 32], P(None, None, 'theta', 'phi'), may hold values from -0.5 to 0.5
Outputs:
- product: float32 [2048, 2, 128, 256], P(('box', 'theta', 'phi'))
The draws below stay inside these ranges and needn't reach their ends.
Inputs may be any that keep to these rules, and one draw needn't show every extreme that they name: `near_ids`: row b lists b itself first, then 12 - 1 further entries; the used ones (before near_count[b]) are distinct other leaf boxes whose index differs from b by at most 8, and some used entry differs by exactly 8. Entries at or after near_count[b] are not used and may repeat b. `near_count`: some leaf box uses all 12 slots. `partners`: row d holds 16 distinct upper boxes other than d whose index differs from d by at most 16; a difference of exactly 16 occurs among used entries. Entries at or after pair_count[d] are not used. `pair_count`: some upper box uses all 16 slots.
All inputs are finite; a program needn't handle non-finite values.
Results may differ from the reference program's by a relative error of at most 0.0055.
Values may be sent and summed in bfloat16 or wider, within the bound.
A program may use at most 128 MiB of HBM per device.

```python
import math
import jax
import jax.numpy as jnp
from jax import lax

P_SIZE = 128
NB = 12
LB_DEV = 8
TL = 8
PL = 16
R = 256
M = 16
NV = 316
KL = 128
TU = 16
PU = 32
NL = 2048
NU = 256
PAR_GROUP = 16


def near_lists(key):
    first, second = jax.random.split(jax.random.fold_in(key, 11))
    boxes = jnp.arange(NL)[:, None]
    places = jnp.arange(2 * LB_DEV)[None, :]
    offset = jnp.where(places < LB_DEV, places - LB_DEV, places - LB_DEV + 1)
    chosen = boxes + offset
    usable = (chosen >= 0) & (chosen < NL)
    scores = jax.random.randint(first, (NL, 2 * LB_DEV), 0, 65536) * 64 + places
    scores = jnp.where(usable, scores, -1 - places)
    scores = scores.at[0, 2 * LB_DEV - 1].set(2 ** 30)
    scores = scores.at[NL - 1, 0].set(2 ** 30)
    ranked, picked = lax.top_k(scores, NB - 1)
    others = jnp.take_along_axis(chosen, picked, axis=1)
    usable_count = jnp.sum(usable.astype(jnp.int32), axis=1)
    others = jnp.where(jnp.arange(NB - 1)[None, :] < usable_count[:, None], others, boxes)
    listed = jnp.concatenate([boxes, others], axis=1).astype(jnp.int32)
    counts = jax.random.randint(second, (NL,), 3, NB + 1)
    counts = jnp.minimum(counts, 1 + usable_count)
    counts = counts.at[NL // 2].set(NB).astype(jnp.int32)
    return (listed, counts)


def pair_lists(key):
    first, second = jax.random.split(jax.random.fold_in(key, 23))
    parents = jnp.arange(NU)[:, None]
    places = jnp.arange(2 * PAR_GROUP)[None, :]
    offset = jnp.where(places < PAR_GROUP, places - PAR_GROUP, places - PAR_GROUP + 1)
    chosen = parents + offset
    usable = (chosen >= 0) & (chosen < NU)
    scores = jax.random.randint(first, (NU, 2 * PAR_GROUP), 0, 65536) * 64 + places
    scores = jnp.where(usable, scores, -1 - places)
    scores = scores.at[0, 2 * PAR_GROUP - 1].set(2 ** 30)
    scores = scores.at[NU - 1, 0].set(2 ** 30)
    ranked, picked = lax.top_k(scores, M)
    listed = jnp.take_along_axis(chosen, picked, axis=1).astype(jnp.int32)
    counts = jax.random.randint(second, (NU,), M // 4, M + 1)
    counts = counts.at[NU // 2].set(M).astype(jnp.int32)
    return (listed, counts)


def draw_near_ids(key, part):
    return near_lists(key)[0]


def draw_near_count(key, part):
    return near_lists(key)[1]


def draw_partners(key, part):
    return pair_lists(key)[0]


def draw_pair_count(key, part):
    return pair_lists(key)[1]


def set_ends(result, rng, smallest, largest):
    spot = [jax.random.randint(jax.random.fold_in(rng, axis), (), 0, length) for axis, length in enumerate(result.shape)]
    main_axis = result.shape.index(max(result.shape))
    next_to = spot[:main_axis] + [(spot[main_axis] + 1) % result.shape[main_axis]] + spot[main_axis + 1:]
    return result.at[tuple(spot)].set(smallest).at[tuple(next_to)].set(largest)


def block_levels(stream_key, shape, pieces, smallest, largest):
    factor_of, own = 1.0, jax.random.fold_in(stream_key, 6)
    for position, parts in pieces:
        steps = jnp.exp(jax.random.uniform(jax.random.fold_in(own, position), (parts,), jnp.float32, smallest / len(pieces), largest / len(pieces)))
        factor_of = factor_of * jnp.repeat(steps, shape[position] // parts).reshape([-1 if axis == position else 1 for axis in range(len(shape))])
    return factor_of


def gaussian(stream_key, dims, scale, reach, shards=(), dtype=jnp.bfloat16):
    level = block_levels(stream_key, dims, shards, -0.22, 0.18) if shards else 1.0
    result = jax.random.normal(stream_key, dims, jnp.float32) * scale * level
    return jnp.minimum(jnp.maximum(result, -reach), reach).astype(dtype)


def setup_inputs(seed: int = 0) -> dict:
    keys = jax.random.split(jax.random.key(seed), 10)
    return {
        "coeffs": gaussian(keys[0], (NL, 2, P_SIZE, R), 1.0, 6.0, ((0, 256),)),
        "near_blocks": gaussian(keys[1], (NL, NB, 2, P_SIZE, P_SIZE), (2 * NB * P_SIZE) ** -0.5, 0.109375, ((0, 256),)),
        "near_ids": draw_near_ids(jax.random.fold_in(keys[9], 71), 0),
        "near_count": draw_near_count(jax.random.fold_in(keys[9], 71), 0),
        "radiation": gaussian(keys[4], (NL, 2, KL, P_SIZE), P_SIZE ** -0.5, 0.5, ((0, 256),)),
        "partners": draw_partners(jax.random.fold_in(keys[9], 71), 0),
        "vector_ids": set_ends(jax.random.randint(keys[6], (NU, M), 0, NV), jax.random.fold_in(keys[6], 1), 0, NV - 1).astype(jnp.int32),
        "pair_count": draw_pair_count(jax.random.fold_in(keys[9], 71), 0),
        "translation": gaussian(keys[8], (NV, 2, TU, PU), ((8 * M) ** -0.5), 0.5, ((2, 4), (3, 4))),
    }


WEIGHT_UP = (-0.0546875, 0.8203125, 0.2734375, -0.0390625)
WEIGHT_DOWN = (-0.0390625, 0.2734375, 0.8203125, -0.0546875)
PHASE_SCALE = 1.3


def lagrange_matrix(upper, columns, rows_in, mode, shift):
    halves = upper // 2
    parity = upper % 2
    column_ids = jnp.arange(columns)
    matrix = jnp.zeros((upper.shape[0], columns), jnp.float32)
    for order in range(4):
        node = halves + parity - 2 + order
        if mode == "wrap":
            node = node % rows_in
        elif mode == "clamp":
            node = jnp.clip(node, 0, rows_in - 1)
        node = node - shift
        weight = jnp.where(parity == 1, WEIGHT_UP[order], WEIGHT_DOWN[order]).astype(jnp.float32)
        matrix = matrix + weight[:, None] * (column_ids[None, :] == node[:, None]).astype(jnp.float32)
    return matrix


def phases(theta_ids, phi_ids, theta_total, phi_total):
    theta = math.pi * (theta_ids.astype(jnp.float32) + 0.5) / theta_total
    azimuth = 2.0 * math.pi * (phi_ids.astype(jnp.float32) + 0.5) / phi_total
    octant = jnp.arange(8)
    sign_x = (2 * (octant % 2) - 1).astype(jnp.float32)[:, None, None]
    sign_y = (2 * ((octant // 2) % 2) - 1).astype(jnp.float32)[:, None, None]
    sign_z = (2 * (octant // 4) - 1).astype(jnp.float32)[:, None, None]
    along_x = (jnp.sin(theta)[:, None] * jnp.cos(azimuth)[None, :])[None]
    along_y = (jnp.sin(theta)[:, None] * jnp.sin(azimuth)[None, :])[None]
    along_z = (jnp.cos(theta)[:, None] * jnp.ones_like(azimuth)[None, :])[None]
    angle = PHASE_SCALE * (sign_x * along_x + sign_y * along_y + sign_z * along_z)
    return jnp.cos(angle), jnp.sin(angle)


def reference(coeffs, near_blocks, near_ids, near_count, radiation, partners, vector_ids, pair_count, translation):
    highest = lax.Precision.HIGHEST
    slot_ids = jnp.arange(NB)

    def near_one(packed):
        blocks, listed, used = packed
        picked = coeffs[listed].astype(jnp.float32)
        in_use = (slot_ids < used).astype(jnp.float32)[:, None, None, None]
        picked = picked * in_use
        blocks = blocks.astype(jnp.float32)
        out_real = jnp.einsum("jpq,jqr->pr", blocks[:, 0], picked[:, 0], precision=highest) - jnp.einsum("jpq,jqr->pr", blocks[:, 1], picked[:, 1], precision=highest)
        out_imag = jnp.einsum("jpq,jqr->pr", blocks[:, 0], picked[:, 1], precision=highest) + jnp.einsum("jpq,jqr->pr", blocks[:, 1], picked[:, 0], precision=highest)
        return jnp.stack([out_real, out_imag])

    near = lax.map(near_one, (near_blocks, near_ids, near_count))

    theta_matrix = lagrange_matrix(jnp.arange(TU), TL, TL, "clamp", 0)
    phi_matrix = lagrange_matrix(jnp.arange(PU), PL, PL, "wrap", 0)
    cosine, sine = phases(jnp.arange(TU), jnp.arange(PU), TU, PU)
    cosine = cosine[:, :, :, None]
    sine = sine[:, :, :, None]
    radiation_groups = radiation.reshape(NU, LB_DEV, 2, KL, P_SIZE)
    coeff_groups = coeffs.reshape(NU, LB_DEV, 2, P_SIZE, R)

    def upward(packed):
        radiating, current = packed
        radiating = radiating.astype(jnp.float32)
        current = current.astype(jnp.float32)
        pattern_real = jnp.einsum("bkp,bpr->bkr", radiating[:, 0], current[:, 0], precision=highest) - jnp.einsum("bkp,bpr->bkr", radiating[:, 1], current[:, 1], precision=highest)
        pattern_imag = jnp.einsum("bkp,bpr->bkr", radiating[:, 0], current[:, 1], precision=highest) + jnp.einsum("bkp,bpr->bkr", radiating[:, 1], current[:, 0], precision=highest)
        leaf_pattern = lax.optimization_barrier(jnp.stack([pattern_real, pattern_imag], axis=1).astype(jnp.bfloat16)).astype(jnp.float32)
        leaf_pattern = leaf_pattern.reshape(LB_DEV, 2, TL, PL, R)
        partial_up = jnp.einsum("ut,bctlr->bculr", theta_matrix, leaf_pattern, precision=highest)
        refined = jnp.einsum("vl,bculr->bcuvr", phi_matrix, partial_up, precision=highest)
        shifted_real = cosine * refined[:, 0] - sine * refined[:, 1]
        shifted_imag = sine * refined[:, 0] + cosine * refined[:, 1]
        return jnp.stack([jnp.sum(shifted_real, axis=0), jnp.sum(shifted_imag, axis=0)]).astype(jnp.bfloat16)

    parent_pattern = lax.map(upward, (radiation_groups, coeff_groups))
    list_slots = jnp.arange(M)

    def translate(packed):
        listed, operators, used = packed
        in_use = (list_slots < used).astype(jnp.float32)[:, None, None, None]
        table = translation[operators].astype(jnp.float32) * in_use
        sources = parent_pattern[listed].astype(jnp.float32)
        field_real = jnp.sum(table[:, 0, :, :, None] * sources[:, 0] - table[:, 1, :, :, None] * sources[:, 1], axis=0)
        field_imag = jnp.sum(table[:, 0, :, :, None] * sources[:, 1] + table[:, 1, :, :, None] * sources[:, 0], axis=0)
        return jnp.stack([field_real, field_imag]).astype(jnp.bfloat16)

    incoming = lax.map(translate, (partners, vector_ids, pair_count))

    def downward(packed):
        arriving, radiating = packed
        arriving = arriving.astype(jnp.float32)
        down_real = cosine * arriving[0][None] + sine * arriving[1][None]
        down_imag = cosine * arriving[1][None] - sine * arriving[0][None]
        spread_down = jnp.stack([down_real, down_imag], axis=1)
        coarse_phi = jnp.einsum("vl,bcuvr->bculr", phi_matrix, spread_down, precision=highest)
        leaf_field = jnp.einsum("ut,bculr->bctlr", theta_matrix, coarse_phi, precision=highest)
        leaf_field = lax.optimization_barrier(leaf_field.astype(jnp.bfloat16)).astype(jnp.float32)
        leaf_field = leaf_field.reshape(LB_DEV, 2, KL, R)
        radiating = radiating.astype(jnp.float32)
        far_real = jnp.einsum("bkp,bkr->bpr", radiating[:, 0], leaf_field[:, 0], precision=highest) + jnp.einsum("bkp,bkr->bpr", radiating[:, 1], leaf_field[:, 1], precision=highest)
        far_imag = jnp.einsum("bkp,bkr->bpr", radiating[:, 0], leaf_field[:, 1], precision=highest) - jnp.einsum("bkp,bkr->bpr", radiating[:, 1], leaf_field[:, 0], precision=highest)
        return jnp.stack([far_real, far_imag], axis=1)

    far = lax.map(downward, (incoming, radiation_groups)).reshape(NL, 2, P_SIZE, R)
    return near + far
```

```python
import functools
import math

import jax
import jax.numpy as jnp
import numpy as np
from jax import lax
from jax.experimental import pallas as pl
from jax.experimental.pallas import tpu as pltpu
from jax.sharding import PartitionSpec as P

MESH = pl.DeviceIdType.MESH
BF = jnp.bfloat16
F32 = jnp.float32

TL, PL, TU, PU = 8, 16, 16, 32
WEIGHT_UP = (-0.0546875, 0.8203125, 0.2734375, -0.0390625)
WEIGHT_DOWN = (-0.0390625, 0.2734375, 0.8203125, -0.0546875)
PHASE_SCALE = 1.3
EARLY = 2
MIDDLE = 4


def lagrange(rows, cols, wrap):
    out = np.zeros((rows, cols), np.float64)
    for u in range(rows):
        i, e = u // 2, u % 2
        for k in range(4):
            node = i + e - 2 + k
            node = node % cols if wrap else min(max(node, 0), cols - 1)
            out[u, node] += (WEIGHT_UP if e == 1 else WEIGHT_DOWN)[k]
    return out


def tables():
    theta, phi = lagrange(TU, TL, False), lagrange(PU, PL, True)
    full = np.einsum("ut,vl->uvtl", theta, phi).reshape(TU, PU, TL * PL)
    a = (math.pi * (np.arange(TU) + 0.5) / TU)[:, None]
    c = (2.0 * math.pi * (np.arange(PU) + 0.5) / PU)[None, :]
    angle = []
    for o in range(4):
        sx, sy, sz = 2 * (o % 2) - 1, 2 * (o // 2 % 2) - 1, 2 * (o // 4) - 1
        angle.append(
            PHASE_SCALE
            * (sx * np.sin(a) * np.cos(c) + sy * np.sin(a) * np.sin(c) + sz * np.cos(a) * np.ones_like(c))
        )
    angle = np.stack(angle, -1)

    def banded(x):
        x = x.reshape(4, 4, 4, 8, -1).transpose(0, 2, 1, 3, 4)
        return x.reshape(512, -1)

    interp, angle = banded(full), banded(angle)
    phase = np.stack([np.cos(angle), np.sin(angle)], -1).reshape(512, 8)
    return interp.astype(np.float32), phase.astype(np.float32)


def split(x):
    high = x.astype(BF)
    return high, (x - high.astype(F32)).astype(BF)


def dot(a, b):
    return jnp.dot(a, b, preferred_element_type=F32)


def stacked(re, im):
    return jnp.concatenate(
        [jnp.concatenate([re, -im], axis=1), jnp.concatenate([im, re], axis=1)], axis=0
    )


def kernel(
    ids_ref, count_ref, x_hbm, blocks_hbm, rad_ref, part_ref, vec_ref, table_ref, interp_ref, phase_ref,
    interp_t_ref, phase_t_ref, out_hbm,
    xb, blocks, w_hi, w_lo, wt, gain, spread, mine, halo, coup, tb, acc, back, returned, rad_t, out,
    x_send, x_recv, a_send, a_recv, h_send, h_recv, b_send, b_recv, local_sem,
):
    box, th, ph = lax.axis_index("box"), lax.axis_index("theta"), lax.axis_index("phi")
    rank = box * 16 + th * 4 + ph
    mine_id = th * 4 + ph

    def ranked(r):
        r = lax.rem(r + 256, 256)
        return {"box": r // 16, "theta": lax.rem(r // 4, 4), "phi": lax.rem(r, 4)}

    def flipped(kb):
        hi, lo = th // 2, lax.rem(th, 2)
        hi = hi + (kb // 2) * (1 - 2 * hi)
        lo = lo + (kb % 2) * (1 - 2 * lo)
        return hi * 2 + lo

    above = {"box": lax.rem(box + 1, 16)}
    below = {"box": lax.rem(box + 15, 16)}

    own_x = pltpu.make_async_copy(x_hbm, xb.at[pl.ds(8, 8)], local_sem.at[0])
    own_x.start()
    own_blocks = pltpu.make_async_copy(blocks_hbm, blocks, local_sem.at[1])
    own_blocks.start()

    barrier = pltpu.get_barrier_semaphore()
    for device in (ranked(rank + 1), ranked(rank - 1), above, below):
        pl.semaphore_signal(barrier, inc=1, device_id=device, device_id_type=MESH)
    for k in range(1, 16):
        device = {"theta": flipped(k // 4), "phi": lax.rem(ph + k % 4, 4)}
        pl.semaphore_signal(barrier, inc=1, device_id=device, device_id_type=MESH)

    for q in range(4):
        for part in range(2):
            cols = pl.ds((2 * q + part) * 128, 128)
            high, low = split(phase_ref[:, 2 * q + part : 2 * q + part + 1] * interp_ref[...])
            w_hi[:, cols] = high
            w_lo[:, cols] = low
    xb[24] = jnp.zeros((256, 256), BF)
    own_x.wait()
    pl.semaphore_wait(barrier, 19)

    def shift(i, way):
        return pltpu.make_async_remote_copy(
            src_ref=xb.at[8 + i],
            dst_ref=xb.at[i if way == 0 else 16 + i],
            send_sem=x_send.at[way, i],
            recv_sem=x_recv.at[way, i],
            device_id=ranked(rank + 1) if way == 0 else ranked(rank - 1),
            device_id_type=MESH,
        )

    def exchange(src, dst, send, recv, kb, kp):
        target_th, target_ph = flipped(kb), lax.rem(ph + kp, 4)
        k = kb * 4 + kp
        return pltpu.make_async_remote_copy(
            src_ref=src.at[target_th * 4 + target_ph],
            dst_ref=dst.at[mine_id],
            send_sem=send.at[k],
            recv_sem=recv.at[k],
            device_id={"theta": target_th, "phi": target_ph},
            device_id_type=MESH,
        )

    def pass_on(k, source, way):
        return pltpu.make_async_remote_copy(
            src_ref=mine.at[source],
            dst_ref=halo.at[way, source],
            send_sem=h_send.at[way, k],
            recv_sem=h_recv.at[way, k],
            device_id=above if way == 0 else below,
            device_id_type=MESH,
        )

    for i in range(EARLY):
        for way in range(2):
            shift(i, way).start()

    for q in range(4):
        low_o = dot(stacked(rad_ref[q, 0], rad_ref[q, 1]), xb[8 + q]).astype(BF).astype(F32)
        high_o = dot(stacked(rad_ref[7 - q, 0], rad_ref[7 - q, 1]), xb[15 - q]).astype(BF).astype(F32)
        total, diff = low_o + high_o, low_o - high_o
        rows, rows2 = pl.ds(q * 256, 128), pl.ds(q * 256 + 128, 128)
        for c, first, second in ((0, total[:128], -diff[128:]), (1, total[128:], diff[:128])):
            high, low = split(first)
            gain[c, rows] = high
            gain[2 + c, rows] = low
            high, low = split(second)
            gain[c, rows2] = high
            gain[2 + c, rows2] = low

    for kb in (3, 2, 1, 0):
        target = flipped(kb)
        rows = pl.ds(pl.multiple_of(target * 128, 128), 128)
        high, low = w_hi[rows], w_lo[rows]
        for c in range(2):
            piece = dot(high, gain[c]) + dot(high, gain[2 + c]) + dot(low, gain[c])
            spread[pl.ds(target * 4, 4), c * 32 : c * 32 + 32] = piece.astype(BF).reshape(4, 32, 256)
        for kp in (2, 1, 3, 0):
            if kb or kp:
                exchange(spread, mine, a_send, a_recv, kb, kp).start()
    mine[mine_id] = spread[mine_id]
    for way in range(2):
        pass_on(0, mine_id, way).start()
    for i in range(EARLY, EARLY + MIDDLE):
        for way in range(2):
            shift(i, way).start()

    hot = (lax.broadcasted_iota(jnp.int32, (316, 256), 0) == vec_ref[...]).astype(F32).astype(BF)
    chosen = dot(table_ref[...], hot).astype(BF)
    lane = lax.broadcasted_iota(jnp.int32, (256, 128), 1)
    row = lax.broadcasted_iota(jnp.int32, (256, 128), 0)
    match = lax.rem(lane, 64) == part_ref[...]
    left = lax.broadcasted_iota(jnp.int32, (32, 128), 1) < 64
    for d in range(16):
        picked = jnp.where(match & (row // 16 == d), 1.0, 0.0).astype(BF)
        both = dot(chosen, picked)
        re, im = both[:32], both[32:]
        coup[64 * d : 64 * d + 32] = jnp.where(left, re, -im).astype(BF)
        coup[64 * d + 32 : 64 * d + 64] = jnp.where(left, im, re).astype(BF)

    def spread_out(n):
        at = lax.broadcasted_iota(jnp.int32, (128, 256), 0)
        to = lax.broadcasted_iota(jnp.int32, (128, 256), 1)
        same = (at // 64 == lax.rem(to // 32, 2)) & (lax.rem(at, 64) == 4 * n + to // 64)
        grow = jnp.where(same, 1.0, 0.0).astype(BF)
        s_row = lax.rem(lax.broadcasted_iota(jnp.int32, (256, 256), 0), 32)
        s_col = lax.rem(lax.broadcasted_iota(jnp.int32, (256, 256), 1), 32)
        for m in range(4):
            wide = dot(coup[256 * m : 256 * m + 256], grow)
            tb[n, 256 * m : 256 * m + 256] = jnp.where(s_row == s_col, wide, 0.0).astype(BF)

    def source_of(kb, kp):
        return flipped(kb) * 4 + lax.rem(ph + 4 - kp, 4)

    def relay(k):
        kb, kp = k // 4, lax.rem(k, 4)
        source = source_of(kb, kp)
        pltpu.make_async_remote_copy(
            src_ref=spread.at[0],
            dst_ref=mine.at[source],
            send_sem=a_send.at[k],
            recv_sem=a_recv.at[k],
            device_id=above,
            device_id_type=MESH,
        ).wait_recv()
        for way in range(2):
            pass_on(k, source, way).start()

    def first(i, carry):
        relay(7 - i)
        spread_out(i)
        return carry

    def second(i, carry):
        relay(15 - i)

        @pl.when(i < 5)
        def _():
            spread_out(7 + i)

        return carry

    lax.fori_loop(0, 7, first, 0)
    lax.fori_loop(0, 8, second, 0)

    for m in range(4):
        rows = slice(256 * m, 256 * m + 256)
        total = dot(tb[4, rows], mine[0:4].reshape(256, 256))
        for n in range(1, 4):
            total = total + dot(tb[4 + n, rows], mine[4 * n : 4 * n + 4].reshape(256, 256))
        acc[rows] = total

    for q in range(4):
        for part in range(2):
            rows = pl.ds((2 * q + part) * 128, 128)
            high, low = split(phase_t_ref[2 * q + part : 2 * q + part + 1, :] * interp_t_ref[...])
            wt[rows, 0:512] = high
            wt[rows, 512:1024] = low
    for o in range(8):
        re, im = rad_ref[o, 0].astype(F32).T.astype(BF), rad_ref[o, 1].astype(F32).T.astype(BF)
        rad_t[o] = stacked(re, -im)

    def arrived(kb):
        for kp in range(4):
            for way in range(2):
                pass_on(kb * 4 + kp, source_of(kb, kp), way).wait_recv()

    def halo_term(kb, rows):
        n = flipped(kb)
        low = dot(tb[n, rows], halo[0, pl.ds(n * 4, 4)].reshape(256, 256))
        high = dot(tb[8 + n, rows], halo[1, pl.ds(n * 4, 4)].reshape(256, 256))
        return low + high

    for kb in (1, 0, 3):
        arrived(kb)
        for m in range(4):
            rows = slice(256 * m, 256 * m + 256)
            acc[rows] += halo_term(kb, rows)
    arrived(2)
    for kb in (3, 2, 1, 0):
        target = flipped(kb)
        rows = pl.ds(pl.multiple_of(target * 256, 256), 256)
        total = acc[rows] + halo_term(2, rows)
        back[pl.ds(target * 4, 4)] = total.astype(BF).reshape(4, 64, 256)
        for kp in (2, 1, 3, 0):
            if kb or kp:
                exchange(back, returned, b_send, b_recv, kb, kp).start()
    returned[mine_id] = back[mine_id]
    for i in range(EARLY + MIDDLE, 8):
        for way in range(2):
            shift(i, way).start()

    for i in range(8):
        for way in range(2):
            shift(i, way).wait_recv()
    own_blocks.wait()

    def near(b, carry):
        left_all, right_all = [], []
        for j in range(12):
            at = jnp.where(j < count_ref[b], ids_ref[b, j] - (rank * 8 - 8), 24)
            left_all.append(stacked(blocks[b, j, 0], blocks[b, j, 1]))
            right_all.append(xb[jnp.clip(at, 0, 24)])
        total = dot(left_all[0], right_all[0])
        for j in range(1, 12):
            total = total + dot(left_all[j], right_all[j])
        out[b] = total
        return carry

    lax.fori_loop(0, 8, near, 0)

    for k in range(1, 16):
        pltpu.make_async_remote_copy(
            src_ref=back.at[0],
            dst_ref=returned.at[source_of(k // 4, k % 4)],
            send_sem=b_send.at[k],
            recv_sem=b_recv.at[k],
            device_id=above,
            device_id_type=MESH,
        ).wait_recv()

    def result(o):
        return pltpu.make_async_copy(out.at[o], out_hbm.at[o], local_sem.at[2 + o])

    field_re = returned[:, 0:32].reshape(512, 256)
    field_im = returned[:, 32:64].reshape(512, 256)
    for q in range(4):
        rows = slice(256 * q, 256 * q + 256)
        re = dot(wt[rows, 0:512], field_re) + dot(wt[rows, 512:1024], field_re)
        im = dot(wt[rows, 0:512], field_im) + dot(wt[rows, 512:1024], field_im)
        cr, sr, ci, si = re[:128], re[128:], im[:128], im[128:]
        leaf = jnp.concatenate([cr + si, ci - sr], axis=0).astype(BF)
        out[q] += dot(rad_t[q], leaf)
        result(q).start()
        leaf = jnp.concatenate([cr - si, ci + sr], axis=0).astype(BF)
        out[7 - q] += dot(rad_t[7 - q], leaf)
        result(7 - q).start()

    for i in range(8):
        for way in range(2):
            shift(i, way).wait_send()
    for k in range(1, 16):
        exchange(spread, mine, a_send, a_recv, k // 4, k % 4).wait_send()
        exchange(back, returned, b_send, b_recv, k // 4, k % 4).wait_send()
    for k in range(16):
        for way in range(2):
            pass_on(k, source_of(k // 4, k % 4), way).wait_send()
    for o in range(8):
        result(o).wait()


def per_device(coeffs, near_blocks, near_ids, near_count, radiation, partners, vector_ids, pair_count, translation):
    interp, phase = tables()
    group = lax.axis_index("box")
    used = jnp.arange(16)[None, :] < pair_count[:, None]
    part = jnp.where(used, partners - (group * 16 - 16), -1).reshape(256, 1)
    vec = vector_ids.reshape(1, 256)
    table = translation.transpose(1, 2, 3, 0).reshape(64, 316)
    vmem, any_, smem = (pl.BlockSpec(memory_space=s) for s in (pltpu.VMEM, pl.ANY, pltpu.SMEM))
    dma = pltpu.SemaphoreType.DMA
    product = pl.pallas_call(
        kernel,
        out_shape=jax.ShapeDtypeStruct((8, 256, 256), F32),
        in_specs=[smem, smem, any_, any_, vmem, vmem, vmem, vmem, vmem, vmem, vmem, vmem],
        out_specs=any_,
        scratch_shapes=[
            pltpu.VMEM((25, 256, 256), BF),
            pltpu.VMEM((8, 12, 2, 128, 128), BF),
            pltpu.VMEM((512, 1024), BF),
            pltpu.VMEM((512, 1024), BF),
            pltpu.VMEM((1024, 1024), BF),
            pltpu.VMEM((4, 1024, 256), BF),
            pltpu.VMEM((16, 64, 256), BF),
            pltpu.VMEM((16, 64, 256), BF),
            pltpu.VMEM((2, 16, 64, 256), BF),
            pltpu.VMEM((1024, 128), BF),
            pltpu.VMEM((12, 1024, 256), BF),
            pltpu.VMEM((1024, 256), F32),
            pltpu.VMEM((16, 64, 256), BF),
            pltpu.VMEM((16, 64, 256), BF),
            pltpu.VMEM((8, 256, 256), BF),
            pltpu.VMEM((8, 256, 256), F32),
            dma((2, 8)),
            dma((2, 8)),
            dma((16,)),
            dma((16,)),
            dma((2, 16)),
            dma((2, 16)),
            dma((16,)),
            dma((16,)),
            dma((10,)),
        ],
        compiler_params=pltpu.CompilerParams(
            collective_id=0, has_side_effects=True, vmem_limit_bytes=56 * 1024 * 1024
        ),
    )(
        near_ids,
        near_count,
        coeffs.reshape(8, 256, 256),
        near_blocks,
        radiation,
        part,
        vec,
        table,
        jnp.asarray(interp),
        jnp.asarray(phase),
        jnp.asarray(np.ascontiguousarray(interp.T)),
        jnp.asarray(np.ascontiguousarray(phase.T)),
    )
    return product.reshape(8, 2, 128, 256)


def solution(mesh):
    ranks = ("box", "theta", "phi")
    in_specs = (
        P(ranks, None, None, None),
        P(ranks, None, None, None, None),
        P(ranks, None),
        P(ranks),
        P(ranks, None, None, None),
        P("box", None),
        P("box", None),
        P("box"),
        P(None, None, "theta", "phi"),
    )
    return jax.shard_map(
        per_device, mesh=mesh, in_specs=in_specs, out_specs=P(ranks, None, None, None), check_vma=False
    )
```

```python
import functools
import math

import jax
import jax.numpy as jnp
import numpy as np
from jax import lax
from jax.experimental import pallas as pl
from jax.experimental.pallas import tpu as pltpu
from jax.sharding import PartitionSpec as P

MESH = pl.DeviceIdType.MESH
BF = jnp.bfloat16
F32 = jnp.float32

TL, PL, TU, PU = 8, 16, 16, 32
WEIGHT_UP = (-0.0546875, 0.8203125, 0.2734375, -0.0390625)
WEIGHT_DOWN = (-0.0390625, 0.2734375, 0.8203125, -0.0546875)
PHASE_SCALE = 1.3
EARLY = 1
MIDDLE = 5
RELAY = True
LIMIT = 56


def lagrange(rows, cols, wrap):
    out = np.zeros((rows, cols), np.float64)
    for u in range(rows):
        i, e = u // 2, u % 2
        for k in range(4):
            node = i + e - 2 + k
            node = node % cols if wrap else min(max(node, 0), cols - 1)
            out[u, node] += (WEIGHT_UP if e == 1 else WEIGHT_DOWN)[k]
    return out


def tables():
    theta, phi = lagrange(TU, TL, False), lagrange(PU, PL, True)
    full = np.einsum("ut,vl->uvtl", theta, phi).reshape(TU, PU, TL * PL)
    a = (math.pi * (np.arange(TU) + 0.5) / TU)[:, None]
    c = (2.0 * math.pi * (np.arange(PU) + 0.5) / PU)[None, :]
    angle = []
    for o in range(4):
        sx, sy, sz = 2 * (o % 2) - 1, 2 * (o // 2 % 2) - 1, 2 * (o // 4) - 1
        angle.append(
            PHASE_SCALE
            * (sx * np.sin(a) * np.cos(c) + sy * np.sin(a) * np.sin(c) + sz * np.cos(a) * np.ones_like(c))
        )
    angle = np.stack(angle, -1)

    def banded(x):
        x = x.reshape(4, 4, 4, 8, -1).transpose(0, 2, 1, 3, 4)
        return x.reshape(512, -1)

    interp, angle = banded(full), banded(angle)
    phase = np.stack([np.cos(angle), np.sin(angle)], -1).reshape(512, 8)
    return interp.astype(np.float32), phase.astype(np.float32)


def split(x):
    high = x.astype(BF)
    return high, (x - high.astype(F32)).astype(BF)


def dot(a, b):
    return jnp.dot(a, b, preferred_element_type=F32)


def stacked(re, im):
    return jnp.concatenate(
        [jnp.concatenate([re, -im], axis=1), jnp.concatenate([im, re], axis=1)], axis=0
    )


def kernel(
    ids_ref, count_ref, used_ref, x_hbm, blocks_hbm, rad_hbm, part_ref, vec_ref, table_hbm, interp_hbm, phase_ref,
    interp_t_hbm, phase_t_ref, out_hbm,
    rad_ref, table_ref, interp_ref, interp_t_ref,
    xb, arrived_x, blocks, w_hi, w_lo, wt, gain, spread, mine, halo, coup, tb, acc, back, returned, rad_t, out,
    x_send, x_recv, a_send, a_recv, h_send, h_recv, b_send, b_recv, local_sem,
):
    box, th, ph = lax.axis_index("box"), lax.axis_index("theta"), lax.axis_index("phi")
    rank = box * 16 + th * 4 + ph
    mine_id = th * 4 + ph

    def ranked(r):
        r = lax.rem(r + 256, 256)
        return {"box": r // 16, "theta": lax.rem(r // 4, 4), "phi": lax.rem(r, 4)}

    def flipped(kb):
        hi, lo = th // 2, lax.rem(th, 2)
        hi = hi + (kb // 2) * (1 - 2 * hi)
        lo = lo + (kb % 2) * (1 - 2 * lo)
        return hi * 2 + lo

    def source_of(kb, kp):
        return flipped(kb) * 4 + lax.rem(ph + 4 - kp, 4)

    above = {"box": lax.rem(box + 1, 16)}
    below = {"box": lax.rem(box + 15, 16)}

    has_above, has_below = box < 15, box > 0
    has_next, has_last = rank < 255, rank > 0
    toward = (has_above, has_below)
    beside = (has_next, has_last)
    corner = RELAY & ((lax.rem(box, 8) == 0) | (lax.rem(box, 8) == 7))

    for way in range(2):

        @pl.when(jnp.logical_not(toward[1 - way]))
        def _():
            halo[way] = jnp.zeros((16, 64, 256), BF)

        @pl.when(jnp.logical_not(beside[1 - way]))
        def _():
            arrived_x[way] = jnp.zeros((8, 256, 256), BF)

    barrier = pltpu.get_barrier_semaphore()

    def greet(device):
        pl.semaphore_signal(barrier, inc=1, device_id=device, device_id_type=MESH)

    for flag, device in (
        (has_next, ranked(rank + 1)),
        (has_last, ranked(rank - 1)),
        (has_above, above),
        (has_below, below),
    ):
        pl.when(flag)(functools.partial(greet, device))
    for flag, device in (
        (corner, {"box": lax.rem(box + 8, 16)}),
        (corner, {"box": box // 8 * 8 + 7 - lax.rem(box, 8)}),
    ):
        pl.when(flag)(functools.partial(greet, device))
    for k in range(1, 16):
        greet({"theta": flipped(k // 4), "phi": lax.rem(ph + k % 4, 4)})

    def load(n, src, dst):
        copy = pltpu.make_async_copy(src, dst, local_sem.at[n])
        copy.start()
        return copy

    own_rad = load(0, rad_hbm, rad_ref)
    own_x = load(1, x_hbm, xb.at[pl.ds(8, 8)])
    own_interp = load(2, interp_hbm, interp_ref)
    own_table = load(3, table_hbm, table_ref)
    own_interp_t = load(4, interp_t_hbm, interp_t_ref)
    own_blocks = load(5, blocks_hbm, blocks)

    xb[24] = jnp.zeros((256, 256), BF)
    def shift(n, way):
        i = 7 - n if way == 0 else n
        return pltpu.make_async_remote_copy(
            src_ref=xb.at[8 + i],
            dst_ref=arrived_x.at[way, i],
            send_sem=x_send.at[way, i],
            recv_sem=x_recv.at[way, i],
            device_id=ranked(rank + 1) if way == 0 else ranked(rank - 1),
            device_id_type=MESH,
        )

    def exchange(src, dst, send, recv, kb, kp):
        target_th, target_ph = flipped(kb), lax.rem(ph + kp, 4)
        k = kb * 4 + kp
        return pltpu.make_async_remote_copy(
            src_ref=src.at[target_th * 4 + target_ph],
            dst_ref=dst.at[mine_id],
            send_sem=send.at[k],
            recv_sem=recv.at[k],
            device_id={"theta": target_th, "phi": target_ph},
            device_id_type=MESH,
        )

    def detoured(k, way):
        at = 7 if way == 0 else 8
        return RELAY & (box == at) & (lax.rem(k, 2) == 1)

    def pass_on(k, source, way):
        off = jnp.where(detoured(k, way), 1, 0)
        slot = way + off * (1 - 2 * way)
        next_box = lax.rem(box + (1 if way == 0 else 15), 16)
        return pltpu.make_async_remote_copy(
            src_ref=mine.at[source],
            dst_ref=halo.at[slot, source],
            send_sem=h_send.at[way, k],
            recv_sem=h_recv.at[slot, k],
            device_id={"box": next_box + off * ((15 if way == 0 else 0) - next_box)},
            device_id_type=MESH,
        )

    def landed(k, source, way):
        return pltpu.make_async_remote_copy(
            src_ref=mine.at[source],
            dst_ref=halo.at[way, source],
            send_sem=h_send.at[way, k],
            recv_sem=h_recv.at[way, k],
            device_id=above if way == 0 else below,
            device_id_type=MESH,
        )

    def hand_over(k, source, way):
        return pltpu.make_async_remote_copy(
            src_ref=halo.at[1 - way, source],
            dst_ref=halo.at[way, source],
            send_sem=h_send.at[way, k],
            recv_sem=h_recv.at[way, k],
            device_id={"box": 8 if way == 0 else 7},
            device_id_type=MESH,
        )

    def detour(k):
        for way in range(2):

            @pl.when(box == (15 if way == 0 else 0))
            def _():
                source = source_of(k // 4, lax.rem(k, 4))
                landed(k, source, 1 - way).wait_recv()
                hand_over(k, source, way).start()

    own_rad.wait()
    own_x.wait()
    for q in range(4):
        low_o = dot(stacked(rad_ref[q, 0], rad_ref[q, 1]), xb[8 + q]).astype(BF).astype(F32)
        high_o = dot(stacked(rad_ref[7 - q, 0], rad_ref[7 - q, 1]), xb[15 - q]).astype(BF).astype(F32)
        total, diff = low_o + high_o, low_o - high_o
        rows, rows2 = pl.ds(q * 256, 128), pl.ds(q * 256 + 128, 128)
        for c, first, second in ((0, total[:128], -diff[128:]), (1, total[128:], diff[:128])):
            high, low = split(first)
            gain[c, rows] = high
            gain[2 + c, rows] = low
            high, low = split(second)
            gain[c, rows2] = high
            gain[2 + c, rows2] = low

    flags = [jnp.where(flag, 1, 0) for flag in toward + beside + (corner, corner)]
    pl.semaphore_wait(barrier, 15 + sum(flags))

    for i in range(EARLY):
        for way in range(2):
            pl.when(beside[way])(shift(i, way).start)

    own_interp.wait()
    for q in range(4):
        for part in range(2):
            cols = pl.ds((2 * q + part) * 128, 128)
            high, low = split(phase_ref[:, 2 * q + part : 2 * q + part + 1] * interp_ref[...])
            w_hi[:, cols] = high
            w_lo[:, cols] = low
    for kb in (3, 2, 1, 0):
        target = flipped(kb)
        rows = pl.ds(pl.multiple_of(target * 128, 128), 128)
        high, low = w_hi[rows], w_lo[rows]
        for c in range(2):
            piece = dot(high, gain[c]) + dot(high, gain[2 + c]) + dot(low, gain[c])
            spread[pl.ds(target * 4, 4), c * 32 : c * 32 + 32] = piece.astype(BF).reshape(4, 32, 256)
        for kp in (2, 1, 3, 0):
            if kb or kp:
                exchange(spread, mine, a_send, a_recv, kb, kp).start()
    mine[mine_id] = spread[mine_id]
    for way in range(2):
        pl.when(toward[way])(pass_on(0, mine_id, way).start)
    for i in range(EARLY, EARLY + MIDDLE):
        for way in range(2):
            pl.when(beside[way])(shift(i, way).start)

    slot = lax.broadcasted_iota(jnp.int32, (1, 16), 1)
    first_source = box * 16 - 16
    vec = jnp.concatenate([vec_ref[d : d + 1] for d in range(16)], axis=1)
    part = jnp.concatenate(
        [jnp.where(slot < used_ref[d], part_ref[d : d + 1] - first_source, -1) for d in range(16)], axis=1
    )
    hot = (lax.broadcasted_iota(jnp.int32, (316, 256), 0) == vec).astype(F32).astype(BF)
    own_table.wait()
    chosen = dot(table_ref[...], hot).astype(BF)
    row = lax.broadcasted_iota(jnp.int32, (128, 256), 0)
    lane = lax.broadcasted_iota(jnp.int32, (128, 256), 1)
    match = lax.rem(row, 64) == part
    left = lax.broadcasted_iota(jnp.int32, (32, 128), 1) < 64
    for d in range(16):
        picked = jnp.where(match & (lane // 16 == d), 1.0, 0.0).astype(BF)
        both = lax.dot_general(chosen, picked, (((1,), (1,)), ((), ())), preferred_element_type=F32)
        re, im = both[:32], both[32:]
        coup[64 * d : 64 * d + 32] = jnp.where(left, re, -im).astype(BF)
        coup[64 * d + 32 : 64 * d + 64] = jnp.where(left, im, re).astype(BF)

    def spread_out(n):
        at = lax.broadcasted_iota(jnp.int32, (128, 256), 0)
        to = lax.broadcasted_iota(jnp.int32, (128, 256), 1)
        same = (at // 64 == lax.rem(to // 32, 2)) & (lax.rem(at, 64) == 4 * n + to // 64)
        grow = jnp.where(same, 1.0, 0.0).astype(BF)
        s_row = lax.rem(lax.broadcasted_iota(jnp.int32, (256, 256), 0), 32)
        s_col = lax.rem(lax.broadcasted_iota(jnp.int32, (256, 256), 1), 32)
        for m in range(4):
            wide = dot(coup[256 * m : 256 * m + 256], grow)
            tb[n, 256 * m : 256 * m + 256] = jnp.where(s_row == s_col, wide, 0.0).astype(BF)

    def relay(k):
        kb, kp = k // 4, lax.rem(k, 4)
        source = source_of(kb, kp)
        pltpu.make_async_remote_copy(
            src_ref=spread.at[0],
            dst_ref=mine.at[source],
            send_sem=a_send.at[k],
            recv_sem=a_recv.at[k],
            device_id=above,
            device_id_type=MESH,
        ).wait_recv()
        for way in range(2):
            pl.when(toward[way])(pass_on(k, source, way).start)

    def first(i, carry):
        relay(7 - i)
        spread_out(i)
        return carry

    def second(i, carry):
        relay(15 - i)
        if RELAY:
            detour(jnp.where(i < 4, 7 - 2 * i, 23 - 2 * i))

        @pl.when(i < 5)
        def _():
            spread_out(7 + i)

        return carry

    lax.fori_loop(0, 7, first, 0)
    lax.fori_loop(0, 8, second, 0)

    for m in range(4):
        rows = slice(256 * m, 256 * m + 256)
        total = dot(tb[4, rows], mine[0:4].reshape(256, 256))
        for n in range(1, 4):
            total = total + dot(tb[4 + n, rows], mine[4 * n : 4 * n + 4].reshape(256, 256))
        acc[rows] = total

    own_interp_t.wait()
    for q in range(4):
        for part in range(2):
            rows = pl.ds((2 * q + part) * 128, 128)
            high, low = split(phase_t_ref[2 * q + part : 2 * q + part + 1, :] * interp_t_ref[...])
            wt[rows, 0:512] = high
            wt[rows, 512:1024] = low
    for o in range(8):
        re, im = rad_ref[o, 0].astype(F32).T.astype(BF), rad_ref[o, 1].astype(F32).T.astype(BF)
        rad_t[o] = stacked(re, -im)

    def arrived(kb):
        for kp in range(4):
            for way in range(2):
                pl.when(toward[1 - way])(landed(kb * 4 + kp, source_of(kb, kp), way).wait_recv)

    def halo_term(kb, rows):
        n = flipped(kb)
        low = dot(tb[n, rows], halo[0, pl.ds(n * 4, 4)].reshape(256, 256))
        high = dot(tb[8 + n, rows], halo[1, pl.ds(n * 4, 4)].reshape(256, 256))
        return low + high

    for kb in (1, 0, 3):
        arrived(kb)
        for m in range(4):
            rows = slice(256 * m, 256 * m + 256)
            acc[rows] += halo_term(kb, rows)
    arrived(2)
    for kb in (3, 2, 1, 0):
        target = flipped(kb)
        rows = pl.ds(pl.multiple_of(target * 256, 256), 256)
        total = acc[rows] + halo_term(2, rows)
        back[pl.ds(target * 4, 4)] = total.astype(BF).reshape(4, 64, 256)
        for kp in (2, 1, 3, 0):
            if kb or kp:
                exchange(back, returned, b_send, b_recv, kb, kp).start()
    returned[mine_id] = back[mine_id]
    for i in range(EARLY + MIDDLE, 8):
        for way in range(2):
            pl.when(beside[way])(shift(i, way).start)

    own_blocks.wait()

    def collect(n):
        for way in range(2):
            i = 7 - n if way == 0 else n
            pl.when(beside[1 - way])(shift(n, way).wait_recv)
            xb[i + 16 * way] = arrived_x[way, i]

    def near(b):
        total = None
        for j in range(12):
            at = jnp.where(j < count_ref[b], ids_ref[b, j] - (rank * 8 - 8), 24)
            term = dot(stacked(blocks[b, j, 0], blocks[b, j, 1]), xb[jnp.clip(at, 0, 24)])
            total = term if j == 0 else total + term
        out[b] = total

    def near_pair(q):
        if q == 3:
            for n in range(4):
                collect(n)
        collect(7 - q)

        def one(n, carry):
            near(q + n * (7 - 2 * q))
            return carry

        lax.fori_loop(0, 2, one, 0)

    for q in (3, 2):
        near_pair(q)

    for k in range(1, 16):
        pltpu.make_async_remote_copy(
            src_ref=back.at[0],
            dst_ref=returned.at[source_of(k // 4, k % 4)],
            send_sem=b_send.at[k],
            recv_sem=b_recv.at[k],
            device_id=above,
            device_id_type=MESH,
        ).wait_recv()

    def result(o):
        return pltpu.make_async_copy(out.at[o], out_hbm.at[o], local_sem.at[6 + o])

    field_re = returned[:, 0:32].reshape(512, 256)
    field_im = returned[:, 32:64].reshape(512, 256)
    for q in (3, 2, 1, 0):
        if q < 2:
            near_pair(q)
        rows = slice(256 * q, 256 * q + 256)
        re = dot(wt[rows, 0:512], field_re) + dot(wt[rows, 512:1024], field_re)
        im = dot(wt[rows, 0:512], field_im) + dot(wt[rows, 512:1024], field_im)
        cr, sr, ci, si = re[:128], re[128:], im[:128], im[128:]
        leaf = jnp.concatenate([cr + si, ci - sr], axis=0).astype(BF)
        out[q] += dot(rad_t[q], leaf)
        result(q).start()
        leaf = jnp.concatenate([cr - si, ci + sr], axis=0).astype(BF)
        out[7 - q] += dot(rad_t[7 - q], leaf)
        result(7 - q).start()

    for i in range(8):
        for way in range(2):
            pl.when(beside[way])(shift(i, way).wait_send)
    for k in range(1, 16):
        exchange(spread, mine, a_send, a_recv, k // 4, k % 4).wait_send()
        exchange(back, returned, b_send, b_recv, k // 4, k % 4).wait_send()
    for k in range(16):
        for way in range(2):
            pl.when(toward[way])(pass_on(k, source_of(k // 4, k % 4), way).wait_send)
            if RELAY and k % 2:
                pl.when(box == (15 if way == 0 else 0))(hand_over(k, source_of(k // 4, k % 4), way).wait_send)
    for o in range(8):
        result(o).wait()


def per_device(coeffs, near_blocks, near_ids, near_count, radiation, partners, vector_ids, pair_count, translation):
    interp, phase = tables()
    table = translation.transpose(1, 2, 3, 0).reshape(64, 316)
    vmem, any_, smem = (pl.BlockSpec(memory_space=s) for s in (pltpu.VMEM, pl.ANY, pltpu.SMEM))
    dma = pltpu.SemaphoreType.DMA
    product = pl.pallas_call(
        kernel,
        out_shape=jax.ShapeDtypeStruct((8, 256, 256), F32),
        in_specs=[smem, smem, smem, any_, any_, any_, vmem, vmem, any_, any_, vmem, any_, vmem],
        out_specs=any_,
        scratch_shapes=[
            pltpu.VMEM((8, 2, 128, 128), BF),
            pltpu.VMEM((64, 316), BF),
            pltpu.VMEM((512, 128), F32),
            pltpu.VMEM((128, 512), F32),
            pltpu.VMEM((25, 256, 256), BF),
            pltpu.VMEM((2, 8, 256, 256), BF),
            pltpu.VMEM((8, 12, 2, 128, 128), BF),
            pltpu.VMEM((512, 1024), BF),
            pltpu.VMEM((512, 1024), BF),
            pltpu.VMEM((1024, 1024), BF),
            pltpu.VMEM((4, 1024, 256), BF),
            pltpu.VMEM((16, 64, 256), BF),
            pltpu.VMEM((16, 64, 256), BF),
            pltpu.VMEM((2, 16, 64, 256), BF),
            pltpu.VMEM((1024, 128), BF),
            pltpu.VMEM((12, 1024, 256), BF),
            pltpu.VMEM((1024, 256), F32),
            pltpu.VMEM((16, 64, 256), BF),
            pltpu.VMEM((16, 64, 256), BF),
            pltpu.VMEM((8, 256, 256), BF),
            pltpu.VMEM((8, 256, 256), F32),
            dma((2, 8)),
            dma((2, 8)),
            dma((16,)),
            dma((16,)),
            dma((2, 16)),
            dma((2, 16)),
            dma((16,)),
            dma((16,)),
            dma((14,)),
        ],
        compiler_params=pltpu.CompilerParams(
            collective_id=0, has_side_effects=True, vmem_limit_bytes=LIMIT * 1024 * 1024
        ),
    )(
        near_ids,
        near_count,
        pair_count,
        coeffs.reshape(8, 256, 256),
        near_blocks,
        radiation,
        partners,
        vector_ids,
        table,
        jnp.asarray(interp),
        jnp.asarray(phase),
        jnp.asarray(np.ascontiguousarray(interp.T)),
        jnp.asarray(np.ascontiguousarray(phase.T)),
    )
    return product.reshape(8, 2, 128, 256)


def solution(mesh):
    ranks = ("box", "theta", "phi")
    in_specs = (
        P(ranks, None, None, None),
        P(ranks, None, None, None, None),
        P(ranks, None),
        P(ranks),
        P(ranks, None, None, None),
        P("box", None),
        P("box", None),
        P("box"),
        P(None, None, "theta", "phi"),
    )
    return jax.shard_map(
        per_device, mesh=mesh, in_specs=in_specs, out_specs=P(ranks, None, None, None), check_vma=False
    )
```

```python
import functools
import math

import jax
import jax.numpy as jnp
import numpy as np
from jax import lax
from jax.experimental import pallas as pl
from jax.experimental.pallas import tpu as pltpu
from jax.sharding import PartitionSpec as P

MESH = pl.DeviceIdType.MESH
BF = jnp.bfloat16
F32 = jnp.float32

TL, PL, TU, PU = 8, 16, 16, 32
WEIGHT_UP = (-0.0546875, 0.8203125, 0.2734375, -0.0390625)
WEIGHT_DOWN = (-0.0390625, 0.2734375, 0.8203125, -0.0546875)
PHASE_SCALE = 1.3
EARLY = 1
MIDDLE = 6
RELAY = True
LIMIT = 40


def lagrange(rows, cols, wrap):
    out = np.zeros((rows, cols), np.float64)
    for u in range(rows):
        i, e = u // 2, u % 2
        for k in range(4):
            node = i + e - 2 + k
            node = node % cols if wrap else min(max(node, 0), cols - 1)
            out[u, node] += (WEIGHT_UP if e == 1 else WEIGHT_DOWN)[k]
    return out


def tables():
    theta, phi = lagrange(TU, TL, False), lagrange(PU, PL, True)
    full = np.einsum("ut,vl->uvtl", theta, phi).reshape(TU, PU, TL * PL)
    a = (math.pi * (np.arange(TU) + 0.5) / TU)[:, None]
    c = (2.0 * math.pi * (np.arange(PU) + 0.5) / PU)[None, :]
    angle = []
    for o in range(4):
        sx, sy, sz = 2 * (o % 2) - 1, 2 * (o // 2 % 2) - 1, 2 * (o // 4) - 1
        angle.append(
            PHASE_SCALE
            * (sx * np.sin(a) * np.cos(c) + sy * np.sin(a) * np.sin(c) + sz * np.cos(a) * np.ones_like(c))
        )
    angle = np.stack(angle, -1)

    def banded(x):
        x = x.reshape(4, 4, 4, 8, -1).transpose(0, 2, 1, 3, 4)
        return x.reshape(512, -1)

    interp, angle = banded(full), banded(angle)
    phase = np.stack([np.cos(angle), np.sin(angle)], -1).reshape(512, 8)
    return interp.astype(np.float32), phase.astype(np.float32)


def split(x):
    high = x.astype(BF)
    return high, (x - high.astype(F32)).astype(BF)


def dot(a, b):
    return jnp.dot(a, b, preferred_element_type=F32)


def stacked(re, im):
    return jnp.concatenate(
        [jnp.concatenate([re, -im], axis=1), jnp.concatenate([im, re], axis=1)], axis=0
    )


def kernel(
    ids_ref, count_ref, used_ref, x_hbm, blocks_hbm, rad_hbm, part_ref, vec_ref, table_hbm, interp_hbm, phase_ref,
    interp_t_hbm, phase_t_ref, out,
    rad_ref, table_ref, interp_ref, interp_t_ref,
    xb, arrived_x, blocks, w_hi, w_lo, wt, gain, spread, mine, halo, coup, tb, acc, back, returned, rad_t,
    x_send, x_recv, a_send, a_recv, h_send, h_recv, b_send, b_recv, local_sem,
):
    box, th, ph = lax.axis_index("box"), lax.axis_index("theta"), lax.axis_index("phi")
    rank = box * 16 + th * 4 + ph
    mine_id = th * 4 + ph

    def ranked(r):
        r = lax.rem(r + 256, 256)
        return {"box": r // 16, "theta": lax.rem(r // 4, 4), "phi": lax.rem(r, 4)}

    def flipped(kb):
        hi, lo = th // 2, lax.rem(th, 2)
        hi = hi + (kb // 2) * (1 - 2 * hi)
        lo = lo + (kb % 2) * (1 - 2 * lo)
        return hi * 2 + lo

    def source_of(kb, kp):
        return flipped(kb) * 4 + lax.rem(ph + 4 - kp, 4)

    above = {"box": lax.rem(box + 1, 16)}
    below = {"box": lax.rem(box + 15, 16)}

    has_above, has_below = box < 15, box > 0
    has_next, has_last = rank < 255, rank > 0
    toward = (has_above, has_below)
    beside = (has_next, has_last)
    corner = RELAY & ((lax.rem(box, 8) == 0) | (lax.rem(box, 8) == 7))

    for way in range(2):

        @pl.when(jnp.logical_not(toward[1 - way]))
        def _():
            halo[way] = jnp.zeros((16, 64, 256), BF)

        @pl.when(jnp.logical_not(beside[1 - way]))
        def _():
            arrived_x[way] = jnp.zeros((8, 256, 256), BF)

    barrier = pltpu.get_barrier_semaphore()

    def greet(device):
        pl.semaphore_signal(barrier, inc=1, device_id=device, device_id_type=MESH)

    for flag, device in (
        (has_next, ranked(rank + 1)),
        (has_last, ranked(rank - 1)),
        (has_above, above),
        (has_below, below),
    ):
        pl.when(flag)(functools.partial(greet, device))
    for flag, device in (
        (corner, {"box": lax.rem(box + 8, 16)}),
        (corner, {"box": box // 8 * 8 + 7 - lax.rem(box, 8)}),
    ):
        pl.when(flag)(functools.partial(greet, device))
    for k in range(1, 16):
        greet({"theta": flipped(k // 4), "phi": lax.rem(ph + k % 4, 4)})

    def load(n, src, dst):
        copy = pltpu.make_async_copy(src, dst, local_sem.at[n])
        copy.start()
        return copy

    own_rad = load(0, rad_hbm, rad_ref)
    own_x = load(1, x_hbm, xb.at[pl.ds(8, 8)])
    own_interp = load(2, interp_hbm, interp_ref)
    own_table = load(3, table_hbm, table_ref)
    own_interp_t = load(4, interp_t_hbm, interp_t_ref)
    own_blocks = load(5, blocks_hbm, blocks)

    xb[24] = jnp.zeros((256, 256), BF)
    def shift(n, way):
        i = 7 - n if way == 0 else n
        return pltpu.make_async_remote_copy(
            src_ref=xb.at[8 + i],
            dst_ref=arrived_x.at[way, i],
            send_sem=x_send.at[way, i],
            recv_sem=x_recv.at[way, i],
            device_id=ranked(rank + 1) if way == 0 else ranked(rank - 1),
            device_id_type=MESH,
        )

    def exchange(src, dst, send, recv, kb, kp):
        target_th, target_ph = flipped(kb), lax.rem(ph + kp, 4)
        k = kb * 4 + kp
        return pltpu.make_async_remote_copy(
            src_ref=src.at[target_th * 4 + target_ph],
            dst_ref=dst.at[mine_id],
            send_sem=send.at[k],
            recv_sem=recv.at[k],
            device_id={"theta": target_th, "phi": target_ph},
            device_id_type=MESH,
        )

    def detoured(k, way):
        at = 7 if way == 0 else 8
        return RELAY & (box == at) & (lax.rem(k, 2) == 1)

    def pass_on(k, source, way):
        off = jnp.where(detoured(k, way), 1, 0)
        slot = way + off * (1 - 2 * way)
        next_box = lax.rem(box + (1 if way == 0 else 15), 16)
        return pltpu.make_async_remote_copy(
            src_ref=mine.at[source],
            dst_ref=halo.at[slot, source],
            send_sem=h_send.at[way, k],
            recv_sem=h_recv.at[slot, k],
            device_id={"box": next_box + off * ((15 if way == 0 else 0) - next_box)},
            device_id_type=MESH,
        )

    def landed(k, source, way):
        return pltpu.make_async_remote_copy(
            src_ref=mine.at[source],
            dst_ref=halo.at[way, source],
            send_sem=h_send.at[way, k],
            recv_sem=h_recv.at[way, k],
            device_id=above if way == 0 else below,
            device_id_type=MESH,
        )

    def hand_over(k, source, way):
        return pltpu.make_async_remote_copy(
            src_ref=halo.at[1 - way, source],
            dst_ref=halo.at[way, source],
            send_sem=h_send.at[way, k],
            recv_sem=h_recv.at[way, k],
            device_id={"box": 8 if way == 0 else 7},
            device_id_type=MESH,
        )

    def detour(k):
        for way in range(2):

            @pl.when(box == (15 if way == 0 else 0))
            def _():
                source = source_of(k // 4, lax.rem(k, 4))
                landed(k, source, 1 - way).wait_recv()
                hand_over(k, source, way).start()

    own_rad.wait()
    own_x.wait()
    for q in range(4):
        low_o = dot(stacked(rad_ref[q, 0], rad_ref[q, 1]), xb[8 + q]).astype(BF).astype(F32)
        high_o = dot(stacked(rad_ref[7 - q, 0], rad_ref[7 - q, 1]), xb[15 - q]).astype(BF).astype(F32)
        total, diff = low_o + high_o, low_o - high_o
        rows, rows2 = pl.ds(q * 256, 128), pl.ds(q * 256 + 128, 128)
        for c, first, second in ((0, total[:128], -diff[128:]), (1, total[128:], diff[:128])):
            high, low = split(first)
            gain[c, rows] = high
            gain[2 + c, rows] = low
            high, low = split(second)
            gain[c, rows2] = high
            gain[2 + c, rows2] = low

    flags = [jnp.where(flag, 1, 0) for flag in toward + beside + (corner, corner)]
    pl.semaphore_wait(barrier, 15 + sum(flags))

    for i in range(EARLY):
        for way in range(2):
            pl.when(beside[way])(shift(i, way).start)

    own_interp.wait()
    for q in range(4):
        for part in range(2):
            cols = pl.ds((2 * q + part) * 128, 128)
            high, low = split(phase_ref[:, 2 * q + part : 2 * q + part + 1] * interp_ref[...])
            w_hi[:, cols] = high
            w_lo[:, cols] = low
    for kb in (3, 2, 1, 0):
        target = flipped(kb)
        rows = pl.ds(pl.multiple_of(target * 128, 128), 128)
        high, low = w_hi[rows], w_lo[rows]
        for c in range(2):
            piece = dot(high, gain[c]) + dot(high, gain[2 + c]) + dot(low, gain[c])
            spread[pl.ds(target * 4, 4), c * 32 : c * 32 + 32] = piece.astype(BF).reshape(4, 32, 256)
        for kp in (2, 1, 3, 0):
            if kb or kp:
                exchange(spread, mine, a_send, a_recv, kb, kp).start()
    mine[mine_id] = spread[mine_id]
    for way in range(2):
        pl.when(toward[way])(pass_on(0, mine_id, way).start)
    for i in range(EARLY, EARLY + MIDDLE):
        for way in range(2):
            pl.when(beside[way])(shift(i, way).start)

    slot = lax.broadcasted_iota(jnp.int32, (1, 16), 1)
    first_source = box * 16 - 16
    vec = jnp.concatenate([vec_ref[d : d + 1] for d in range(16)], axis=1)
    part = jnp.concatenate(
        [jnp.where(slot < used_ref[d], part_ref[d : d + 1] - first_source, -1) for d in range(16)], axis=1
    )
    hot = (lax.broadcasted_iota(jnp.int32, (316, 256), 0) == vec).astype(F32).astype(BF)
    own_table.wait()
    chosen = dot(table_ref[...], hot).astype(BF)
    row = lax.broadcasted_iota(jnp.int32, (128, 256), 0)
    lane = lax.broadcasted_iota(jnp.int32, (128, 256), 1)
    match = lax.rem(row, 64) == part
    left = lax.broadcasted_iota(jnp.int32, (32, 128), 1) < 64
    for d in range(16):
        picked = jnp.where(match & (lane // 16 == d), 1.0, 0.0).astype(BF)
        both = lax.dot_general(chosen, picked, (((1,), (1,)), ((), ())), preferred_element_type=F32)
        re, im = both[:32], both[32:]
        coup[64 * d : 64 * d + 32] = jnp.where(left, re, -im).astype(BF)
        coup[64 * d + 32 : 64 * d + 64] = jnp.where(left, im, re).astype(BF)

    def spread_out(n):
        at = lax.broadcasted_iota(jnp.int32, (128, 256), 0)
        to = lax.broadcasted_iota(jnp.int32, (128, 256), 1)
        same = (at // 64 == lax.rem(to // 32, 2)) & (lax.rem(at, 64) == 4 * n + to // 64)
        grow = jnp.where(same, 1.0, 0.0).astype(BF)
        s_row = lax.rem(lax.broadcasted_iota(jnp.int32, (256, 256), 0), 32)
        s_col = lax.rem(lax.broadcasted_iota(jnp.int32, (256, 256), 1), 32)
        for m in range(4):
            wide = dot(coup[256 * m : 256 * m + 256], grow)
            tb[n, 256 * m : 256 * m + 256] = jnp.where(s_row == s_col, wide, 0.0).astype(BF)

    def relay(k):
        kb, kp = k // 4, lax.rem(k, 4)
        source = source_of(kb, kp)
        pltpu.make_async_remote_copy(
            src_ref=spread.at[0],
            dst_ref=mine.at[source],
            send_sem=a_send.at[k],
            recv_sem=a_recv.at[k],
            device_id=above,
            device_id_type=MESH,
        ).wait_recv()
        for way in range(2):
            pl.when(toward[way])(pass_on(k, source, way).start)

    def first(i, carry):
        relay(7 - i)
        if RELAY:
            pl.when((i >= 2) & (lax.rem(i, 2) == 0))(functools.partial(detour, 9 - i))
        spread_out(i)
        return carry

    def second(i, carry):
        relay(15 - i)
        if RELAY:
            pl.when(lax.rem(i, 2) == 0)(functools.partial(detour, jnp.where(i == 0, 1, 17 - i)))

        @pl.when(i < 5)
        def _():
            spread_out(7 + i)

        return carry

    lax.fori_loop(0, 7, first, 0)
    lax.fori_loop(0, 8, second, 0)
    if RELAY:
        detour(9)

    for m in range(4):
        rows = slice(256 * m, 256 * m + 256)
        total = dot(tb[4, rows], mine[0:4].reshape(256, 256))
        for n in range(1, 4):
            total = total + dot(tb[4 + n, rows], mine[4 * n : 4 * n + 4].reshape(256, 256))
        acc[rows] = total

    own_interp_t.wait()
    for q in range(4):
        for part in range(2):
            rows = pl.ds((2 * q + part) * 128, 128)
            high, low = split(phase_t_ref[2 * q + part : 2 * q + part + 1, :] * interp_t_ref[...])
            wt[rows, 0:512] = high
            wt[rows, 512:1024] = low
    for o in range(8):
        re, im = rad_ref[o, 0].astype(F32).T.astype(BF), rad_ref[o, 1].astype(F32).T.astype(BF)
        rad_t[o] = stacked(re, -im)

    def arrived(kb):
        for kp in range(4):
            for way in range(2):
                pl.when(toward[1 - way])(landed(kb * 4 + kp, source_of(kb, kp), way).wait_recv)

    def halo_term(kb, rows):
        n = flipped(kb)
        low = dot(tb[n, rows], halo[0, pl.ds(n * 4, 4)].reshape(256, 256))
        high = dot(tb[8 + n, rows], halo[1, pl.ds(n * 4, 4)].reshape(256, 256))
        return low + high

    for kb in (1, 0, 3):
        arrived(kb)
        for m in range(4):
            rows = slice(256 * m, 256 * m + 256)
            acc[rows] += halo_term(kb, rows)
    arrived(2)
    for kb in (3, 2, 1, 0):
        target = flipped(kb)
        rows = pl.ds(pl.multiple_of(target * 256, 256), 256)
        total = acc[rows] + halo_term(2, rows)
        back[pl.ds(target * 4, 4)] = total.astype(BF).reshape(4, 64, 256)
        for kp in (2, 1, 3, 0):
            if kb or kp:
                exchange(back, returned, b_send, b_recv, kb, kp).start()
    returned[mine_id] = back[mine_id]
    for i in range(EARLY + MIDDLE, 8):
        for way in range(2):
            pl.when(beside[way])(shift(i, way).start)

    own_blocks.wait()

    def collect(n):
        for way in range(2):
            i = 7 - n if way == 0 else n
            pl.when(beside[1 - way])(shift(n, way).wait_recv)
            xb[i + 16 * way] = arrived_x[way, i]

    def near(b, first_term):
        total = None
        for j in range(12):
            at = jnp.where(j < count_ref[b], ids_ref[b, j] - (rank * 8 - 8), 24)
            term = dot(stacked(blocks[b, j, 0], blocks[b, j, 1]), xb[jnp.clip(at, 0, 24)])
            total = term if j == 0 else total + term
        if first_term:
            out[b] = total
        else:
            out[b] += total

    def near_pair(q):
        if q == 3:
            for n in range(4):
                collect(n)
        collect(7 - q)

        def one(n, carry):
            near(q + n * (7 - 2 * q), q > 1)
            return carry

        lax.fori_loop(0, 2, one, 0)

    for q in (3, 2):
        near_pair(q)

    for k in range(1, 16):
        pltpu.make_async_remote_copy(
            src_ref=back.at[0],
            dst_ref=returned.at[source_of(k // 4, k % 4)],
            send_sem=b_send.at[k],
            recv_sem=b_recv.at[k],
            device_id=above,
            device_id_type=MESH,
        ).wait_recv()

    field_re = returned[:, 0:32].reshape(512, 256)
    field_im = returned[:, 32:64].reshape(512, 256)
    for q in (3, 2, 1, 0):
        rows = slice(256 * q, 256 * q + 256)
        re = dot(wt[rows, 0:512], field_re) + dot(wt[rows, 512:1024], field_re)
        im = dot(wt[rows, 0:512], field_im) + dot(wt[rows, 512:1024], field_im)
        cr, sr, ci, si = re[:128], re[128:], im[:128], im[128:]
        for o, leaf in ((q, (cr + si, ci - sr)), (7 - q, (cr - si, ci + sr))):
            far = dot(rad_t[o], jnp.concatenate(leaf, axis=0).astype(BF))
            if q > 1:
                out[o] += far
            else:
                out[o] = far
    for q in (1, 0):
        near_pair(q)

    for i in range(8):
        for way in range(2):
            pl.when(beside[way])(shift(i, way).wait_send)
    for k in range(1, 16):
        exchange(spread, mine, a_send, a_recv, k // 4, k % 4).wait_send()
        exchange(back, returned, b_send, b_recv, k // 4, k % 4).wait_send()
    for k in range(16):
        for way in range(2):
            pl.when(toward[way])(pass_on(k, source_of(k // 4, k % 4), way).wait_send)
            if RELAY and k % 2:
                pl.when(box == (15 if way == 0 else 0))(hand_over(k, source_of(k // 4, k % 4), way).wait_send)


def per_device(coeffs, near_blocks, near_ids, near_count, radiation, partners, vector_ids, pair_count, translation):
    interp, phase = tables()
    table = translation.transpose(1, 2, 3, 0).reshape(64, 316)
    vmem, any_, smem = (pl.BlockSpec(memory_space=s) for s in (pltpu.VMEM, pl.ANY, pltpu.SMEM))
    dma = pltpu.SemaphoreType.DMA
    product = pl.pallas_call(
        kernel,
        out_shape=jax.ShapeDtypeStruct((8, 256, 256), F32),
        in_specs=[smem, smem, smem, any_, any_, any_, vmem, vmem, any_, any_, vmem, any_, vmem],
        out_specs=vmem,
        scratch_shapes=[
            pltpu.VMEM((8, 2, 128, 128), BF),
            pltpu.VMEM((64, 316), BF),
            pltpu.VMEM((512, 128), F32),
            pltpu.VMEM((128, 512), F32),
            pltpu.VMEM((25, 256, 256), BF),
            pltpu.VMEM((2, 8, 256, 256), BF),
            pltpu.VMEM((8, 12, 2, 128, 128), BF),
            pltpu.VMEM((512, 1024), BF),
            pltpu.VMEM((512, 1024), BF),
            pltpu.VMEM((1024, 1024), BF),
            pltpu.VMEM((4, 1024, 256), BF),
            pltpu.VMEM((16, 64, 256), BF),
            pltpu.VMEM((16, 64, 256), BF),
            pltpu.VMEM((2, 16, 64, 256), BF),
            pltpu.VMEM((1024, 128), BF),
            pltpu.VMEM((12, 1024, 256), BF),
            pltpu.VMEM((1024, 256), F32),
            pltpu.VMEM((16, 64, 256), BF),
            pltpu.VMEM((16, 64, 256), BF),
            pltpu.VMEM((8, 256, 256), BF),
            dma((2, 8)),
            dma((2, 8)),
            dma((16,)),
            dma((16,)),
            dma((2, 16)),
            dma((2, 16)),
            dma((16,)),
            dma((16,)),
            dma((6,)),
        ],
        compiler_params=pltpu.CompilerParams(
            collective_id=0, has_side_effects=True, vmem_limit_bytes=LIMIT * 1024 * 1024
        ),
    )(
        *(
            pltpu.with_memory_space_constraint(value, pltpu.HBM)
            for value in (
                near_ids,
                near_count,
                pair_count,
                coeffs.reshape(8, 256, 256),
                near_blocks,
                radiation,
                partners,
                vector_ids,
                table,
                jnp.asarray(interp),
                jnp.asarray(phase),
                jnp.asarray(np.ascontiguousarray(interp.T)),
                jnp.asarray(np.ascontiguousarray(phase.T)),
            )
        )
    )
    return product.reshape(8, 2, 128, 256)


def solution(mesh):
    ranks = ("box", "theta", "phi")
    in_specs = (
        P(ranks, None, None, None),
        P(ranks, None, None, None, None),
        P(ranks, None),
        P(ranks),
        P(ranks, None, None, None),
        P("box", None),
        P("box", None),
        P("box"),
        P(None, None, "theta", "phi"),
    )
    return jax.shard_map(
        per_device, mesh=mesh, in_specs=in_specs, out_specs=P(ranks, None, None, None), check_vma=False
    )
```

```python
import functools
import math

import jax
import jax.numpy as jnp
import numpy as np
from jax import lax
from jax.experimental import pallas as pl
from jax.experimental.pallas import tpu as pltpu
from jax.sharding import PartitionSpec as P

MESH = pl.DeviceIdType.MESH
BF = jnp.bfloat16
F32 = jnp.float32

TL, PL, TU, PU = 8, 16, 16, 32
WEIGHT_UP = (-0.0546875, 0.8203125, 0.2734375, -0.0390625)
WEIGHT_DOWN = (-0.0390625, 0.2734375, 0.8203125, -0.0546875)
PHASE_SCALE = 1.3
EARLY = 1
MIDDLE = 6
RELAY = True
LIMIT = 40


def lagrange(rows, cols, wrap):
    out = np.zeros((rows, cols), np.float64)
    for u in range(rows):
        i, e = u // 2, u % 2
        for k in range(4):
            node = i + e - 2 + k
            node = node % cols if wrap else min(max(node, 0), cols - 1)
            out[u, node] += (WEIGHT_UP if e == 1 else WEIGHT_DOWN)[k]
    return out


def tables():
    theta, phi = lagrange(TU, TL, False), lagrange(PU, PL, True)
    full = np.einsum("ut,vl->uvtl", theta, phi).reshape(TU, PU, TL * PL)
    a = (math.pi * (np.arange(TU) + 0.5) / TU)[:, None]
    c = (2.0 * math.pi * (np.arange(PU) + 0.5) / PU)[None, :]
    angle = []
    for o in range(4):
        sx, sy, sz = 2 * (o % 2) - 1, 2 * (o // 2 % 2) - 1, 2 * (o // 4) - 1
        angle.append(
            PHASE_SCALE
            * (sx * np.sin(a) * np.cos(c) + sy * np.sin(a) * np.sin(c) + sz * np.cos(a) * np.ones_like(c))
        )
    angle = np.stack(angle, -1)

    def banded(x):
        x = x.reshape(4, 4, 4, 8, -1).transpose(0, 2, 1, 3, 4)
        return x.reshape(512, -1)

    interp, angle = banded(full), banded(angle)
    phase = np.stack([np.cos(angle), np.sin(angle)], -1).reshape(512, 8)
    return interp.astype(np.float32), phase.astype(np.float32)


def split(x):
    high = x.astype(BF)
    return high, (x - high.astype(F32)).astype(BF)


def dot(a, b):
    return jnp.dot(a, b, preferred_element_type=F32)


def stacked(re, im):
    return jnp.concatenate(
        [jnp.concatenate([re, -im], axis=1), jnp.concatenate([im, re], axis=1)], axis=0
    )


def kernel(
    ids_hbm, count_hbm, used_hbm, x_hbm, blocks_hbm, rad_hbm, part_hbm, vec_hbm, table_hbm, interp_hbm, phase_hbm,
    interp_t_hbm, phase_t_hbm, out,
    ids_ref, count_ref, used_ref, rad_ref, table_ref, interp_ref, interp_t_ref, part_ref, vec_ref, phase_ref, phase_t_ref,
    xb, arrived_x, blocks, w_hi, w_lo, wt, gain, spread, mine, halo, coup, tb, acc, back, returned, rad_t,
    x_send, x_recv, a_send, a_recv, h_send, h_recv, b_send, b_recv, local_sem,
):
    box, th, ph = lax.axis_index("box"), lax.axis_index("theta"), lax.axis_index("phi")
    rank = box * 16 + th * 4 + ph
    mine_id = th * 4 + ph

    def ranked(r):
        r = lax.rem(r + 256, 256)
        return {"box": r // 16, "theta": lax.rem(r // 4, 4), "phi": lax.rem(r, 4)}

    def flipped(kb):
        hi, lo = th // 2, lax.rem(th, 2)
        hi = hi + (kb // 2) * (1 - 2 * hi)
        lo = lo + (kb % 2) * (1 - 2 * lo)
        return hi * 2 + lo

    def source_of(kb, kp):
        return flipped(kb) * 4 + lax.rem(ph + 4 - kp, 4)

    above = {"box": lax.rem(box + 1, 16)}
    below = {"box": lax.rem(box + 15, 16)}

    has_above, has_below = box < 15, box > 0
    has_next, has_last = rank < 255, rank > 0
    toward = (has_above, has_below)
    beside = (has_next, has_last)
    corner = RELAY & ((lax.rem(box, 8) == 0) | (lax.rem(box, 8) == 7))

    for way in range(2):

        @pl.when(jnp.logical_not(toward[1 - way]))
        def _():
            halo[way] = jnp.zeros((16, 64, 256), BF)

        @pl.when(jnp.logical_not(beside[1 - way]))
        def _():
            arrived_x[way] = jnp.zeros((8, 256, 256), BF)

    barrier = pltpu.get_barrier_semaphore()

    def greet(device):
        pl.semaphore_signal(barrier, inc=1, device_id=device, device_id_type=MESH)

    for flag, device in (
        (has_next, ranked(rank + 1)),
        (has_last, ranked(rank - 1)),
        (has_above, above),
        (has_below, below),
    ):
        pl.when(flag)(functools.partial(greet, device))
    for flag, device in (
        (corner, {"box": lax.rem(box + 8, 16)}),
        (corner, {"box": box // 8 * 8 + 7 - lax.rem(box, 8)}),
    ):
        pl.when(flag)(functools.partial(greet, device))
    for k in range(1, 16):
        greet({"theta": flipped(k // 4), "phi": lax.rem(ph + k % 4, 4)})

    def load(n, src, dst):
        copy = pltpu.make_async_copy(src, dst, local_sem.at[n])
        copy.start()
        return copy

    own_rad = load(0, rad_hbm, rad_ref)
    own_x = load(1, x_hbm, xb.at[pl.ds(8, 8)])
    own_interp = load(2, interp_hbm, interp_ref)
    own_phase = load(8, phase_hbm, phase_ref)
    own_table = load(3, table_hbm, table_ref)
    own_interp_t = load(4, interp_t_hbm, interp_t_ref)
    own_part = load(6, part_hbm, part_ref)
    own_vec = load(7, vec_hbm, vec_ref)
    own_ids = load(10, ids_hbm, ids_ref)
    own_count = load(11, count_hbm, count_ref)
    own_used = load(12, used_hbm, used_ref)
    own_phase_t = load(9, phase_t_hbm, phase_t_ref)
    own_blocks = load(5, blocks_hbm, blocks)

    xb[24] = jnp.zeros((256, 256), BF)
    def shift(n, way):
        i = 7 - n if way == 0 else n
        return pltpu.make_async_remote_copy(
            src_ref=xb.at[8 + i],
            dst_ref=arrived_x.at[way, i],
            send_sem=x_send.at[way, i],
            recv_sem=x_recv.at[way, i],
            device_id=ranked(rank + 1) if way == 0 else ranked(rank - 1),
            device_id_type=MESH,
        )

    def exchange(src, dst, send, recv, kb, kp):
        target_th, target_ph = flipped(kb), lax.rem(ph + kp, 4)
        k = kb * 4 + kp
        return pltpu.make_async_remote_copy(
            src_ref=src.at[target_th * 4 + target_ph],
            dst_ref=dst.at[mine_id],
            send_sem=send.at[k],
            recv_sem=recv.at[k],
            device_id={"theta": target_th, "phi": target_ph},
            device_id_type=MESH,
        )

    def detoured(k, way):
        at = 7 if way == 0 else 8
        return RELAY & (box == at) & (lax.rem(k, 2) == 1)

    def pass_on(k, source, way):
        off = jnp.where(detoured(k, way), 1, 0)
        slot = way + off * (1 - 2 * way)
        next_box = lax.rem(box + (1 if way == 0 else 15), 16)
        return pltpu.make_async_remote_copy(
            src_ref=mine.at[source],
            dst_ref=halo.at[slot, source],
            send_sem=h_send.at[way, k],
            recv_sem=h_recv.at[slot, k],
            device_id={"box": next_box + off * ((15 if way == 0 else 0) - next_box)},
            device_id_type=MESH,
        )

    def landed(k, source, way):
        return pltpu.make_async_remote_copy(
            src_ref=mine.at[source],
            dst_ref=halo.at[way, source],
            send_sem=h_send.at[way, k],
            recv_sem=h_recv.at[way, k],
            device_id=above if way == 0 else below,
            device_id_type=MESH,
        )

    def hand_over(k, source, way):
        return pltpu.make_async_remote_copy(
            src_ref=halo.at[1 - way, source],
            dst_ref=halo.at[way, source],
            send_sem=h_send.at[way, k],
            recv_sem=h_recv.at[way, k],
            device_id={"box": 8 if way == 0 else 7},
            device_id_type=MESH,
        )

    def detour(k):
        for way in range(2):

            @pl.when(box == (15 if way == 0 else 0))
            def _():
                source = source_of(k // 4, lax.rem(k, 4))
                landed(k, source, 1 - way).wait_recv()
                hand_over(k, source, way).start()

    own_rad.wait()
    own_x.wait()
    for q in range(4):
        low_o = dot(stacked(rad_ref[q, 0], rad_ref[q, 1]), xb[8 + q]).astype(BF).astype(F32)
        high_o = dot(stacked(rad_ref[7 - q, 0], rad_ref[7 - q, 1]), xb[15 - q]).astype(BF).astype(F32)
        total, diff = low_o + high_o, low_o - high_o
        rows, rows2 = pl.ds(q * 256, 128), pl.ds(q * 256 + 128, 128)
        for c, first, second in ((0, total[:128], -diff[128:]), (1, total[128:], diff[:128])):
            high, low = split(first)
            gain[c, rows] = high
            gain[2 + c, rows] = low
            high, low = split(second)
            gain[c, rows2] = high
            gain[2 + c, rows2] = low

    flags = [jnp.where(flag, 1, 0) for flag in toward + beside + (corner, corner)]
    pl.semaphore_wait(barrier, 15 + sum(flags))

    for i in range(EARLY):
        for way in range(2):
            pl.when(beside[way])(shift(i, way).start)

    own_interp.wait()
    own_phase.wait()
    for q in range(4):
        for part in range(2):
            cols = pl.ds((2 * q + part) * 128, 128)
            high, low = split(phase_ref[:, 2 * q + part : 2 * q + part + 1] * interp_ref[...])
            w_hi[:, cols] = high
            w_lo[:, cols] = low
    for kb in (3, 2, 1, 0):
        target = flipped(kb)
        rows = pl.ds(pl.multiple_of(target * 128, 128), 128)
        high, low = w_hi[rows], w_lo[rows]
        for c in range(2):
            piece = dot(high, gain[c]) + dot(high, gain[2 + c]) + dot(low, gain[c])
            spread[pl.ds(target * 4, 4), c * 32 : c * 32 + 32] = piece.astype(BF).reshape(4, 32, 256)
        for kp in (2, 1, 3, 0):
            if kb or kp:
                exchange(spread, mine, a_send, a_recv, kb, kp).start()
    mine[mine_id] = spread[mine_id]
    for way in range(2):
        pl.when(toward[way])(pass_on(0, mine_id, way).start)
    for i in range(EARLY, EARLY + MIDDLE):
        for way in range(2):
            pl.when(beside[way])(shift(i, way).start)

    own_part.wait()
    own_vec.wait()
    own_used.wait()
    own_ids.wait()
    own_count.wait()
    slot = lax.broadcasted_iota(jnp.int32, (1, 16), 1)
    first_source = box * 16 - 16
    vec = jnp.concatenate([vec_ref[d : d + 1] for d in range(16)], axis=1)
    part = jnp.concatenate(
        [jnp.where(slot < used_ref[d], part_ref[d : d + 1] - first_source, -1) for d in range(16)], axis=1
    )
    hot = (lax.broadcasted_iota(jnp.int32, (316, 256), 0) == vec).astype(F32).astype(BF)
    own_table.wait()
    chosen = dot(table_ref[...], hot).astype(BF)
    row = lax.broadcasted_iota(jnp.int32, (128, 256), 0)
    lane = lax.broadcasted_iota(jnp.int32, (128, 256), 1)
    match = lax.rem(row, 64) == part
    left = lax.broadcasted_iota(jnp.int32, (32, 128), 1) < 64
    for d in range(16):
        picked = jnp.where(match & (lane // 16 == d), 1.0, 0.0).astype(BF)
        both = lax.dot_general(chosen, picked, (((1,), (1,)), ((), ())), preferred_element_type=F32)
        re, im = both[:32], both[32:]
        coup[64 * d : 64 * d + 32] = jnp.where(left, re, -im).astype(BF)
        coup[64 * d + 32 : 64 * d + 64] = jnp.where(left, im, re).astype(BF)

    def spread_out(n):
        at = lax.broadcasted_iota(jnp.int32, (128, 256), 0)
        to = lax.broadcasted_iota(jnp.int32, (128, 256), 1)
        same = (at // 64 == lax.rem(to // 32, 2)) & (lax.rem(at, 64) == 4 * n + to // 64)
        grow = jnp.where(same, 1.0, 0.0).astype(BF)
        s_row = lax.rem(lax.broadcasted_iota(jnp.int32, (256, 256), 0), 32)
        s_col = lax.rem(lax.broadcasted_iota(jnp.int32, (256, 256), 1), 32)
        for m in range(4):
            wide = dot(coup[256 * m : 256 * m + 256], grow)
            tb[n, 256 * m : 256 * m + 256] = jnp.where(s_row == s_col, wide, 0.0).astype(BF)

    def relay(k):
        kb, kp = k // 4, lax.rem(k, 4)
        source = source_of(kb, kp)
        pltpu.make_async_remote_copy(
            src_ref=spread.at[0],
            dst_ref=mine.at[source],
            send_sem=a_send.at[k],
            recv_sem=a_recv.at[k],
            device_id=above,
            device_id_type=MESH,
        ).wait_recv()
        for way in range(2):
            pl.when(toward[way])(pass_on(k, source, way).start)

    def first(i, carry):
        relay(7 - i)
        if RELAY:
            pl.when((i >= 2) & (lax.rem(i, 2) == 0))(functools.partial(detour, 9 - i))
        spread_out(i)
        return carry

    def second(i, carry):
        relay(15 - i)
        if RELAY:
            pl.when(lax.rem(i, 2) == 0)(functools.partial(detour, jnp.where(i == 0, 1, 17 - i)))

        @pl.when(i < 5)
        def _():
            spread_out(7 + i)

        return carry

    lax.fori_loop(0, 7, first, 0)
    lax.fori_loop(0, 8, second, 0)
    if RELAY:
        detour(9)

    for m in range(4):
        rows = slice(256 * m, 256 * m + 256)
        total = dot(tb[4, rows], mine[0:4].reshape(256, 256))
        for n in range(1, 4):
            total = total + dot(tb[4 + n, rows], mine[4 * n : 4 * n + 4].reshape(256, 256))
        acc[rows] = total

    own_interp_t.wait()
    own_phase_t.wait()
    for q in range(4):
        for part in range(2):
            rows = pl.ds((2 * q + part) * 128, 128)
            high, low = split(phase_t_ref[2 * q + part : 2 * q + part + 1, :] * interp_t_ref[...])
            wt[rows, 0:512] = high
            wt[rows, 512:1024] = low
    for o in range(8):
        re, im = rad_ref[o, 0].astype(F32).T.astype(BF), rad_ref[o, 1].astype(F32).T.astype(BF)
        rad_t[o] = stacked(re, -im)

    def arrived(kb):
        for kp in range(4):
            for way in range(2):
                pl.when(toward[1 - way])(landed(kb * 4 + kp, source_of(kb, kp), way).wait_recv)

    def halo_term(kb, rows):
        n = flipped(kb)
        low = dot(tb[n, rows], halo[0, pl.ds(n * 4, 4)].reshape(256, 256))
        high = dot(tb[8 + n, rows], halo[1, pl.ds(n * 4, 4)].reshape(256, 256))
        return low + high

    for kb in (1, 0, 3):
        arrived(kb)
        for m in range(4):
            rows = slice(256 * m, 256 * m + 256)
            acc[rows] += halo_term(kb, rows)
    arrived(2)
    for kb in (3, 2, 1, 0):
        target = flipped(kb)
        rows = pl.ds(pl.multiple_of(target * 256, 256), 256)
        total = acc[rows] + halo_term(2, rows)
        back[pl.ds(target * 4, 4)] = total.astype(BF).reshape(4, 64, 256)
        for kp in (2, 1, 3, 0):
            if kb or kp:
                exchange(back, returned, b_send, b_recv, kb, kp).start()
    returned[mine_id] = back[mine_id]
    for i in range(EARLY + MIDDLE, 8):
        for way in range(2):
            pl.when(beside[way])(shift(i, way).start)

    own_blocks.wait()

    def collect(n):
        for way in range(2):
            i = 7 - n if way == 0 else n
            pl.when(beside[1 - way])(shift(n, way).wait_recv)
            xb[i + 16 * way] = arrived_x[way, i]

    def near(b, first_term):
        total = None
        for j in range(12):
            at = jnp.where(j < count_ref[b], ids_ref[b, j] - (rank * 8 - 8), 24)
            term = dot(stacked(blocks[b, j, 0], blocks[b, j, 1]), xb[jnp.clip(at, 0, 24)])
            total = term if j == 0 else total + term
        if first_term:
            out[b] = total
        else:
            out[b] += total

    def near_pair(q):
        if q == 3:
            for n in range(4):
                collect(n)
        collect(7 - q)

        def one(n, carry):
            near(q + n * (7 - 2 * q), q > 1)
            return carry

        lax.fori_loop(0, 2, one, 0)

    for q in (3, 2):
        near_pair(q)

    for k in range(1, 16):
        pltpu.make_async_remote_copy(
            src_ref=back.at[0],
            dst_ref=returned.at[source_of(k // 4, k % 4)],
            send_sem=b_send.at[k],
            recv_sem=b_recv.at[k],
            device_id=above,
            device_id_type=MESH,
        ).wait_recv()

    field_re = returned[:, 0:32].reshape(512, 256)
    field_im = returned[:, 32:64].reshape(512, 256)
    for q in (3, 2, 1, 0):
        rows = slice(256 * q, 256 * q + 256)
        re = dot(wt[rows, 0:512], field_re) + dot(wt[rows, 512:1024], field_re)
        im = dot(wt[rows, 0:512], field_im) + dot(wt[rows, 512:1024], field_im)
        cr, sr, ci, si = re[:128], re[128:], im[:128], im[128:]
        for o, leaf in ((q, (cr + si, ci - sr)), (7 - q, (cr - si, ci + sr))):
            far = dot(rad_t[o], jnp.concatenate(leaf, axis=0).astype(BF))
            if q > 1:
                out[o] += far
            else:
                out[o] = far
    for q in (1, 0):
        near_pair(q)

    for i in range(8):
        for way in range(2):
            pl.when(beside[way])(shift(i, way).wait_send)
    for k in range(1, 16):
        exchange(spread, mine, a_send, a_recv, k // 4, k % 4).wait_send()
        exchange(back, returned, b_send, b_recv, k // 4, k % 4).wait_send()
    for k in range(16):
        for way in range(2):
            pl.when(toward[way])(pass_on(k, source_of(k // 4, k % 4), way).wait_send)
            if RELAY and k % 2:
                pl.when(box == (15 if way == 0 else 0))(hand_over(k, source_of(k // 4, k % 4), way).wait_send)


def per_device(coeffs, near_blocks, near_ids, near_count, radiation, partners, vector_ids, pair_count, translation):
    interp, phase = tables()
    table = translation.transpose(1, 2, 3, 0).reshape(64, 316)
    vmem, any_, smem = (pl.BlockSpec(memory_space=s) for s in (pltpu.VMEM, pl.ANY, pltpu.SMEM))
    dma = pltpu.SemaphoreType.DMA
    product = pl.pallas_call(
        kernel,
        out_shape=jax.ShapeDtypeStruct((8, 256, 256), F32),
        in_specs=[any_] * 13,
        out_specs=vmem,
        scratch_shapes=[
            pltpu.SMEM((8, 12), jnp.int32),
            pltpu.SMEM((8,), jnp.int32),
            pltpu.SMEM((16,), jnp.int32),
            pltpu.VMEM((8, 2, 128, 128), BF),
            pltpu.VMEM((64, 316), BF),
            pltpu.VMEM((512, 128), F32),
            pltpu.VMEM((128, 512), F32),
            pltpu.VMEM((16, 16), jnp.int32),
            pltpu.VMEM((16, 16), jnp.int32),
            pltpu.VMEM((512, 8), F32),
            pltpu.VMEM((8, 512), F32),
            pltpu.VMEM((25, 256, 256), BF),
            pltpu.VMEM((2, 8, 256, 256), BF),
            pltpu.VMEM((8, 12, 2, 128, 128), BF),
            pltpu.VMEM((512, 1024), BF),
            pltpu.VMEM((512, 1024), BF),
            pltpu.VMEM((1024, 1024), BF),
            pltpu.VMEM((4, 1024, 256), BF),
            pltpu.VMEM((16, 64, 256), BF),
            pltpu.VMEM((16, 64, 256), BF),
            pltpu.VMEM((2, 16, 64, 256), BF),
            pltpu.VMEM((1024, 128), BF),
            pltpu.VMEM((12, 1024, 256), BF),
            pltpu.VMEM((1024, 256), F32),
            pltpu.VMEM((16, 64, 256), BF),
            pltpu.VMEM((16, 64, 256), BF),
            pltpu.VMEM((8, 256, 256), BF),
            dma((2, 8)),
            dma((2, 8)),
            dma((16,)),
            dma((16,)),
            dma((2, 16)),
            dma((2, 16)),
            dma((16,)),
            dma((16,)),
            dma((13,)),
        ],
        compiler_params=pltpu.CompilerParams(
            collective_id=0, has_side_effects=True, vmem_limit_bytes=LIMIT * 1024 * 1024
        ),
    )(
        *(
            pltpu.with_memory_space_constraint(value, pltpu.HBM)
            for value in (
                near_ids,
                near_count,
                pair_count,
                coeffs.reshape(8, 256, 256),
                near_blocks,
                radiation,
                partners,
                vector_ids,
                table,
                jnp.asarray(interp),
                jnp.asarray(phase),
                jnp.asarray(np.ascontiguousarray(interp.T)),
                jnp.asarray(np.ascontiguousarray(phase.T)),
            )
        )
    )
    return product.reshape(8, 2, 128, 256)


def solution(mesh):
    ranks = ("box", "theta", "phi")
    in_specs = (
        P(ranks, None, None, None),
        P(ranks, None, None, None, None),
        P(ranks, None),
        P(ranks),
        P(ranks, None, None, None),
        P("box", None),
        P("box", None),
        P("box"),
        P(None, None, "theta", "phi"),
    )
    return jax.shard_map(
        per_device, mesh=mesh, in_specs=in_specs, out_specs=P(ranks, None, None, None), check_vma=False
    )
```

```python
import functools
import math

import jax
import jax.numpy as jnp
import numpy as np
from jax import lax
from jax.experimental import pallas as pl
from jax.experimental.pallas import tpu as pltpu
from jax.sharding import PartitionSpec as P

MESH = pl.DeviceIdType.MESH
BF = jnp.bfloat16
F32 = jnp.float32

TL, PL, TU, PU = 8, 16, 16, 32
WEIGHT_UP = (-0.0546875, 0.8203125, 0.2734375, -0.0390625)
WEIGHT_DOWN = (-0.0390625, 0.2734375, 0.8203125, -0.0546875)
PHASE_SCALE = 1.3
EARLY = 0
MIDDLE = 7
RELAY = True
LIMIT = 40


def lagrange(rows, cols, wrap):
    out = np.zeros((rows, cols), np.float64)
    for u in range(rows):
        i, e = u // 2, u % 2
        for k in range(4):
            node = i + e - 2 + k
            node = node % cols if wrap else min(max(node, 0), cols - 1)
            out[u, node] += (WEIGHT_UP if e == 1 else WEIGHT_DOWN)[k]
    return out


def tables():
    theta, phi = lagrange(TU, TL, False), lagrange(PU, PL, True)
    full = np.einsum("ut,vl->uvtl", theta, phi).reshape(TU, PU, TL * PL)
    a = (math.pi * (np.arange(TU) + 0.5) / TU)[:, None]
    c = (2.0 * math.pi * (np.arange(PU) + 0.5) / PU)[None, :]
    angle = []
    for o in range(4):
        sx, sy, sz = 2 * (o % 2) - 1, 2 * (o // 2 % 2) - 1, 2 * (o // 4) - 1
        angle.append(
            PHASE_SCALE
            * (sx * np.sin(a) * np.cos(c) + sy * np.sin(a) * np.sin(c) + sz * np.cos(a) * np.ones_like(c))
        )
    angle = np.stack(angle, -1)

    def banded(x):
        x = x.reshape(4, 4, 4, 8, -1).transpose(0, 2, 1, 3, 4)
        return x.reshape(512, -1)

    interp, angle = banded(full), banded(angle)
    phase = np.stack([np.cos(angle), np.sin(angle)], -1).reshape(512, 8)
    return interp.astype(np.float32), phase.astype(np.float32)


def split(x):
    high = x.astype(BF)
    return high, (x - high.astype(F32)).astype(BF)


def dot(a, b):
    return jnp.dot(a, b, preferred_element_type=F32)


def stacked(re, im):
    return jnp.concatenate(
        [jnp.concatenate([re, -im], axis=1), jnp.concatenate([im, re], axis=1)], axis=0
    )


def kernel(
    ids_hbm, count_hbm, used_hbm, x_hbm, blocks_hbm, rad_hbm, part_hbm, vec_hbm, table_hbm, interp_hbm, phase_hbm,
    interp_t_hbm, phase_t_hbm, out,
    ids_ref, count_ref, used_ref, rad_ref, table_ref, interp_ref, interp_t_ref, part_ref, vec_ref, phase_ref, phase_t_ref,
    xb, arrived_x, blocks, w_hi, w_lo, wt, gain, spread, mine, halo, coup, tb, acc, back, returned, rad_t,
    x_send, x_recv, a_send, a_recv, h_send, h_recv, b_send, b_recv, local_sem,
):
    box, th, ph = lax.axis_index("box"), lax.axis_index("theta"), lax.axis_index("phi")
    rank = box * 16 + th * 4 + ph
    mine_id = th * 4 + ph

    def ranked(r):
        r = lax.rem(r + 256, 256)
        return {"box": r // 16, "theta": lax.rem(r // 4, 4), "phi": lax.rem(r, 4)}

    def flipped(kb):
        hi, lo = th // 2, lax.rem(th, 2)
        hi = hi + (kb // 2) * (1 - 2 * hi)
        lo = lo + (kb % 2) * (1 - 2 * lo)
        return hi * 2 + lo

    def source_of(kb, kp):
        return flipped(kb) * 4 + lax.rem(ph + 4 - kp, 4)

    above = {"box": lax.rem(box + 1, 16)}
    below = {"box": lax.rem(box + 15, 16)}

    has_above, has_below = box < 15, box > 0
    has_next, has_last = rank < 255, rank > 0
    toward = (has_above, has_below)
    beside = (has_next, has_last)
    corner = RELAY & ((lax.rem(box, 8) == 0) | (lax.rem(box, 8) == 7))

    for way in range(2):

        @pl.when(jnp.logical_not(toward[1 - way]))
        def _():
            halo[way] = jnp.zeros((16, 64, 256), BF)

        @pl.when(jnp.logical_not(beside[1 - way]))
        def _():
            arrived_x[way] = jnp.zeros((8, 256, 256), BF)

    barrier = pltpu.get_barrier_semaphore()

    def greet(device):
        pl.semaphore_signal(barrier, inc=1, device_id=device, device_id_type=MESH)

    for flag, device in (
        (has_next, ranked(rank + 1)),
        (has_last, ranked(rank - 1)),
        (has_above, above),
        (has_below, below),
    ):
        pl.when(flag)(functools.partial(greet, device))
    for flag, device in (
        (corner, {"box": lax.rem(box + 8, 16)}),
        (corner, {"box": box // 8 * 8 + 7 - lax.rem(box, 8)}),
    ):
        pl.when(flag)(functools.partial(greet, device))
    for k in range(1, 16):
        greet({"theta": flipped(k // 4), "phi": lax.rem(ph + k % 4, 4)})

    def load(n, src, dst):
        copy = pltpu.make_async_copy(src, dst, local_sem.at[n])
        copy.start()
        return copy

    own_rad = load(0, rad_hbm, rad_ref)
    own_x = load(1, x_hbm, xb.at[pl.ds(8, 8)])
    own_interp = load(2, interp_hbm, interp_ref)
    own_phase = load(8, phase_hbm, phase_ref)
    own_table = load(3, table_hbm, table_ref)
    own_interp_t = load(4, interp_t_hbm, interp_t_ref)
    own_part = load(6, part_hbm, part_ref)
    own_vec = load(7, vec_hbm, vec_ref)
    own_ids = load(10, ids_hbm, ids_ref)
    own_count = load(11, count_hbm, count_ref)
    own_used = load(12, used_hbm, used_ref)
    own_phase_t = load(9, phase_t_hbm, phase_t_ref)
    own_blocks = load(5, blocks_hbm, blocks)

    xb[24] = jnp.zeros((256, 256), BF)
    def shift(n, way):
        i = 7 - n if way == 0 else n
        return pltpu.make_async_remote_copy(
            src_ref=xb.at[8 + i],
            dst_ref=arrived_x.at[way, i],
            send_sem=x_send.at[way, i],
            recv_sem=x_recv.at[way, i],
            device_id=ranked(rank + 1) if way == 0 else ranked(rank - 1),
            device_id_type=MESH,
        )

    def exchange(src, dst, send, recv, kb, kp):
        target_th, target_ph = flipped(kb), lax.rem(ph + kp, 4)
        k = kb * 4 + kp
        return pltpu.make_async_remote_copy(
            src_ref=src.at[target_th * 4 + target_ph],
            dst_ref=dst.at[mine_id],
            send_sem=send.at[k],
            recv_sem=recv.at[k],
            device_id={"theta": target_th, "phi": target_ph},
            device_id_type=MESH,
        )

    def detoured(k, way):
        at = 7 if way == 0 else 8
        return RELAY & (box == at) & (lax.rem(k, 2) == 1)

    def pass_on(k, source, way):
        off = jnp.where(detoured(k, way), 1, 0)
        slot = way + off * (1 - 2 * way)
        next_box = lax.rem(box + (1 if way == 0 else 15), 16)
        return pltpu.make_async_remote_copy(
            src_ref=mine.at[source],
            dst_ref=halo.at[slot, source],
            send_sem=h_send.at[way, k],
            recv_sem=h_recv.at[slot, k],
            device_id={"box": next_box + off * ((15 if way == 0 else 0) - next_box)},
            device_id_type=MESH,
        )

    def landed(k, source, way):
        return pltpu.make_async_remote_copy(
            src_ref=mine.at[source],
            dst_ref=halo.at[way, source],
            send_sem=h_send.at[way, k],
            recv_sem=h_recv.at[way, k],
            device_id=above if way == 0 else below,
            device_id_type=MESH,
        )

    def hand_over(k, source, way):
        return pltpu.make_async_remote_copy(
            src_ref=halo.at[1 - way, source],
            dst_ref=halo.at[way, source],
            send_sem=h_send.at[way, k],
            recv_sem=h_recv.at[way, k],
            device_id={"box": 8 if way == 0 else 7},
            device_id_type=MESH,
        )

    def detour(k):
        for way in range(2):

            @pl.when(box == (15 if way == 0 else 0))
            def _():
                source = source_of(k // 4, lax.rem(k, 4))
                landed(k, source, 1 - way).wait_recv()
                hand_over(k, source, way).start()

    own_rad.wait()
    own_x.wait()
    for q in range(4):
        low_o = dot(stacked(rad_ref[q, 0], rad_ref[q, 1]), xb[8 + q]).astype(BF).astype(F32)
        high_o = dot(stacked(rad_ref[7 - q, 0], rad_ref[7 - q, 1]), xb[15 - q]).astype(BF).astype(F32)
        total, diff = low_o + high_o, low_o - high_o
        rows, rows2 = pl.ds(q * 256, 128), pl.ds(q * 256 + 128, 128)
        for c, first, second in ((0, total[:128], -diff[128:]), (1, total[128:], diff[:128])):
            high, low = split(first)
            gain[c, rows] = high
            gain[2 + c, rows] = low
            high, low = split(second)
            gain[c, rows2] = high
            gain[2 + c, rows2] = low

    flags = [jnp.where(flag, 1, 0) for flag in toward + beside + (corner, corner)]
    pl.semaphore_wait(barrier, 15 + sum(flags))

    for i in range(EARLY):
        for way in range(2):
            pl.when(beside[way])(shift(i, way).start)

    own_interp.wait()
    own_phase.wait()
    for q in range(4):
        for part in range(2):
            cols = pl.ds((2 * q + part) * 128, 128)
            high, low = split(phase_ref[:, 2 * q + part : 2 * q + part + 1] * interp_ref[...])
            w_hi[:, cols] = high
            w_lo[:, cols] = low
    for kb in (3, 2, 1, 0):
        target = flipped(kb)
        rows = pl.ds(pl.multiple_of(target * 128, 128), 128)
        high, low = w_hi[rows], w_lo[rows]
        for c in range(2):
            piece = dot(high, gain[c]) + dot(high, gain[2 + c]) + dot(low, gain[c])
            spread[pl.ds(target * 4, 4), c * 32 : c * 32 + 32] = piece.astype(BF).reshape(4, 32, 256)
        for kp in (2, 1, 3, 0):
            if kb or kp:
                exchange(spread, mine, a_send, a_recv, kb, kp).start()
    mine[mine_id] = spread[mine_id]
    for way in range(2):
        pl.when(toward[way])(pass_on(0, mine_id, way).start)
    for i in range(EARLY, EARLY + MIDDLE):
        for way in range(2):
            pl.when(beside[way])(shift(i, way).start)

    own_part.wait()
    own_vec.wait()
    own_used.wait()
    own_ids.wait()
    own_count.wait()
    slot = lax.broadcasted_iota(jnp.int32, (1, 16), 1)
    first_source = box * 16 - 16
    vec = jnp.concatenate([vec_ref[d : d + 1] for d in range(16)], axis=1)
    part = jnp.concatenate(
        [jnp.where(slot < used_ref[d], part_ref[d : d + 1] - first_source, -1) for d in range(16)], axis=1
    )
    hot = (lax.broadcasted_iota(jnp.int32, (316, 256), 0) == vec).astype(F32).astype(BF)
    own_table.wait()
    chosen = dot(table_ref[...], hot).astype(BF)
    row = lax.broadcasted_iota(jnp.int32, (128, 256), 0)
    lane = lax.broadcasted_iota(jnp.int32, (128, 256), 1)
    match = lax.rem(row, 64) == part
    left = lax.broadcasted_iota(jnp.int32, (32, 128), 1) < 64
    for d in range(16):
        picked = jnp.where(match & (lane // 16 == d), 1.0, 0.0).astype(BF)
        both = lax.dot_general(chosen, picked, (((1,), (1,)), ((), ())), preferred_element_type=F32)
        re, im = both[:32], both[32:]
        coup[64 * d : 64 * d + 32] = jnp.where(left, re, -im).astype(BF)
        coup[64 * d + 32 : 64 * d + 64] = jnp.where(left, im, re).astype(BF)

    def spread_out(n):
        at = lax.broadcasted_iota(jnp.int32, (128, 256), 0)
        to = lax.broadcasted_iota(jnp.int32, (128, 256), 1)
        same = (at // 64 == lax.rem(to // 32, 2)) & (lax.rem(at, 64) == 4 * n + to // 64)
        grow = jnp.where(same, 1.0, 0.0).astype(BF)
        s_row = lax.rem(lax.broadcasted_iota(jnp.int32, (256, 256), 0), 32)
        s_col = lax.rem(lax.broadcasted_iota(jnp.int32, (256, 256), 1), 32)
        for m in range(4):
            wide = dot(coup[256 * m : 256 * m + 256], grow)
            tb[n, 256 * m : 256 * m + 256] = jnp.where(s_row == s_col, wide, 0.0).astype(BF)

    def relay(k):
        kb, kp = k // 4, lax.rem(k, 4)
        source = source_of(kb, kp)
        pltpu.make_async_remote_copy(
            src_ref=spread.at[0],
            dst_ref=mine.at[source],
            send_sem=a_send.at[k],
            recv_sem=a_recv.at[k],
            device_id=above,
            device_id_type=MESH,
        ).wait_recv()
        for way in range(2):
            pl.when(toward[way])(pass_on(k, source, way).start)

    def first(i, carry):
        relay(7 - i)
        if RELAY:
            pl.when((i >= 2) & (lax.rem(i, 2) == 0))(functools.partial(detour, 9 - i))
        spread_out(i)
        return carry

    def second(i, carry):
        relay(15 - i)
        if RELAY:
            pl.when(lax.rem(i, 2) == 0)(functools.partial(detour, jnp.where(i == 0, 1, 17 - i)))

        @pl.when(i < 5)
        def _():
            spread_out(7 + i)

        return carry

    lax.fori_loop(0, 7, first, 0)
    lax.fori_loop(0, 8, second, 0)
    if RELAY:
        detour(9)

    for m in range(4):
        rows = slice(256 * m, 256 * m + 256)
        total = dot(tb[4, rows], mine[0:4].reshape(256, 256))
        for n in range(1, 4):
            total = total + dot(tb[4 + n, rows], mine[4 * n : 4 * n + 4].reshape(256, 256))
        acc[rows] = total

    own_interp_t.wait()
    own_phase_t.wait()
    for q in range(4):
        for part in range(2):
            rows = pl.ds((2 * q + part) * 128, 128)
            high, low = split(phase_t_ref[2 * q + part : 2 * q + part + 1, :] * interp_t_ref[...])
            wt[rows, 0:512] = high
            wt[rows, 512:1024] = low
    for o in range(8):
        re, im = rad_ref[o, 0].astype(F32).T.astype(BF), rad_ref[o, 1].astype(F32).T.astype(BF)
        rad_t[o] = stacked(re, -im)

    def arrived(kb):
        for kp in range(4):
            for way in range(2):
                pl.when(toward[1 - way])(landed(kb * 4 + kp, source_of(kb, kp), way).wait_recv)

    def halo_term(kb, rows):
        n = flipped(kb)
        low = dot(tb[n, rows], halo[0, pl.ds(n * 4, 4)].reshape(256, 256))
        high = dot(tb[8 + n, rows], halo[1, pl.ds(n * 4, 4)].reshape(256, 256))
        return low + high

    for kb in (1, 0, 3):
        arrived(kb)
        for m in range(4):
            rows = slice(256 * m, 256 * m + 256)
            acc[rows] += halo_term(kb, rows)
    arrived(2)
    for kb in (3, 2, 1, 0):
        target = flipped(kb)
        rows = pl.ds(pl.multiple_of(target * 256, 256), 256)
        total = acc[rows] + halo_term(2, rows)
        back[pl.ds(target * 4, 4)] = total.astype(BF).reshape(4, 64, 256)
        for kp in (2, 1, 3, 0):
            if kb or kp:
                exchange(back, returned, b_send, b_recv, kb, kp).start()
    returned[mine_id] = back[mine_id]
    for i in range(EARLY + MIDDLE, 8):
        for way in range(2):
            pl.when(beside[way])(shift(i, way).start)

    own_blocks.wait()

    def collect(n):
        for way in range(2):
            i = 7 - n if way == 0 else n
            pl.when(beside[1 - way])(shift(n, way).wait_recv)
            xb[i + 16 * way] = arrived_x[way, i]

    def near(b, first_term):
        total = None
        for j in range(12):
            at = jnp.where(j < count_ref[b], ids_ref[b, j] - (rank * 8 - 8), 24)
            term = dot(stacked(blocks[b, j, 0], blocks[b, j, 1]), xb[jnp.clip(at, 0, 24)])
            total = term if j == 0 else total + term
        if first_term:
            out[b] = total
        else:
            out[b] += total

    def near_pair(q):
        if q == 3:
            for n in range(4):
                collect(n)
        collect(7 - q)

        def one(n, carry):
            near(q + n * (7 - 2 * q), q > 1)
            return carry

        lax.fori_loop(0, 2, one, 0)

    for q in (3, 2):
        near_pair(q)

    for k in range(1, 16):
        pltpu.make_async_remote_copy(
            src_ref=back.at[0],
            dst_ref=returned.at[source_of(k // 4, k % 4)],
            send_sem=b_send.at[k],
            recv_sem=b_recv.at[k],
            device_id=above,
            device_id_type=MESH,
        ).wait_recv()

    field_re = returned[:, 0:32].reshape(512, 256)
    field_im = returned[:, 32:64].reshape(512, 256)
    for q in (3, 2, 1, 0):
        rows = slice(256 * q, 256 * q + 256)
        re = dot(wt[rows, 0:512], field_re) + dot(wt[rows, 512:1024], field_re)
        im = dot(wt[rows, 0:512], field_im) + dot(wt[rows, 512:1024], field_im)
        cr, sr, ci, si = re[:128], re[128:], im[:128], im[128:]
        for o, leaf in ((q, (cr + si, ci - sr)), (7 - q, (cr - si, ci + sr))):
            far = dot(rad_t[o], jnp.concatenate(leaf, axis=0).astype(BF))
            if q > 1:
                out[o] += far
            else:
                out[o] = far
    for q in (1, 0):
        near_pair(q)

    for i in range(8):
        for way in range(2):
            pl.when(beside[way])(shift(i, way).wait_send)
    for k in range(1, 16):
        exchange(spread, mine, a_send, a_recv, k // 4, k % 4).wait_send()
        exchange(back, returned, b_send, b_recv, k // 4, k % 4).wait_send()
    for k in range(16):
        for way in range(2):
            pl.when(toward[way])(pass_on(k, source_of(k // 4, k % 4), way).wait_send)
            if RELAY and k % 2:
                pl.when(box == (15 if way == 0 else 0))(hand_over(k, source_of(k // 4, k % 4), way).wait_send)


def per_device(coeffs, near_blocks, near_ids, near_count, radiation, partners, vector_ids, pair_count, translation):
    interp, phase = tables()
    table = translation.transpose(1, 2, 3, 0).reshape(64, 316)
    vmem, any_, smem = (pl.BlockSpec(memory_space=s) for s in (pltpu.VMEM, pl.ANY, pltpu.SMEM))
    dma = pltpu.SemaphoreType.DMA
    product = pl.pallas_call(
        kernel,
        out_shape=jax.ShapeDtypeStruct((8, 256, 256), F32),
        in_specs=[any_] * 13,
        out_specs=vmem,
        scratch_shapes=[
            pltpu.SMEM((8, 12), jnp.int32),
            pltpu.SMEM((8,), jnp.int32),
            pltpu.SMEM((16,), jnp.int32),
            pltpu.VMEM((8, 2, 128, 128), BF),
            pltpu.VMEM((64, 316), BF),
            pltpu.VMEM((512, 128), F32),
            pltpu.VMEM((128, 512), F32),
            pltpu.VMEM((16, 16), jnp.int32),
            pltpu.VMEM((16, 16), jnp.int32),
            pltpu.VMEM((512, 8), F32),
            pltpu.VMEM((8, 512), F32),
            pltpu.VMEM((25, 256, 256), BF),
            pltpu.VMEM((2, 8, 256, 256), BF),
            pltpu.VMEM((8, 12, 2, 128, 128), BF),
            pltpu.VMEM((512, 1024), BF),
            pltpu.VMEM((512, 1024), BF),
            pltpu.VMEM((1024, 1024), BF),
            pltpu.VMEM((4, 1024, 256), BF),
            pltpu.VMEM((16, 64, 256), BF),
            pltpu.VMEM((16, 64, 256), BF),
            pltpu.VMEM((2, 16, 64, 256), BF),
            pltpu.VMEM((1024, 128), BF),
            pltpu.VMEM((12, 1024, 256), BF),
            pltpu.VMEM((1024, 256), F32),
            pltpu.VMEM((16, 64, 256), BF),
            pltpu.VMEM((16, 64, 256), BF),
            pltpu.VMEM((8, 256, 256), BF),
            dma((2, 8)),
            dma((2, 8)),
            dma((16,)),
            dma((16,)),
            dma((2, 16)),
            dma((2, 16)),
            dma((16,)),
            dma((16,)),
            dma((13,)),
        ],
        compiler_params=pltpu.CompilerParams(
            collective_id=0, has_side_effects=True, vmem_limit_bytes=LIMIT * 1024 * 1024
        ),
    )(
        *(
            pltpu.with_memory_space_constraint(value, pltpu.HBM)
            for value in (
                near_ids,
                near_count,
                pair_count,
                coeffs.reshape(8, 256, 256),
                near_blocks,
                radiation,
                partners,
                vector_ids,
                table,
                jnp.asarray(interp),
                jnp.asarray(phase),
                jnp.asarray(np.ascontiguousarray(interp.T)),
                jnp.asarray(np.ascontiguousarray(phase.T)),
            )
        )
    )
    return product.reshape(8, 2, 128, 256)


def solution(mesh):
    ranks = ("box", "theta", "phi")
    in_specs = (
        P(ranks, None, None, None),
        P(ranks, None, None, None, None),
        P(ranks, None),
        P(ranks),
        P(ranks, None, None, None),
        P("box", None),
        P("box", None),
        P("box"),
        P(None, None, "theta", "phi"),
    )
    return jax.shard_map(
        per_device, mesh=mesh, in_specs=in_specs, out_specs=P(ranks, None, None, None), check_vma=False
    )
```
